128 devices in a mesh: grp: 16 (over z, x), loc: 8 (over y, core).
Axes of the slice: x: 4, y: 4, z: 4, core: 2. Of those that a mesh axis runs over, the one named last changes fastest.
Arguments:
- acts: bfloat16 [16384, 2048], P(('grp', 'loc')), may hold values from -6 to 6
- out_grad: bfloat16 [16384, 2048], P(('grp', 'loc')), may hold values from -6 to 6
- expert_ids: int32 [16384, 8], P(('grp', 'loc')), may hold values from 0 to 127, all different within a row; in each aligned block of 128 rows (0 to 127, 128 to 255, ...) at most 9 rows name the same one
- gate_vals: bfloat16 [16384, 8], P(('grp', 'loc')), may hold values from 0.049804688 to 0.5
- w_gate: bfloat16 [128, 2048, 768], P(('grp', 'loc')), may hold values from -0.125 to 0.125
- w_up: bfloat16 [128, 2048, 768], P(('grp', 'loc')), may hold values from -0.125 to 0.125
- w_down: bfloat16 [128, 768, 2048], P(('grp', 'loc')), may hold values from -0.21875 to 0.21875
Outputs:
- grad_acts: bfloat16 [16384, 2048], P(('grp', 'loc'))
- grad_gates: bfloat16 [16384, 8], P(('grp', 'loc'))
- grad_w_gate: bfloat16 [128, 2048, 768], P(('grp', 'loc'))
- grad_w_up: bfloat16 [128, 2048, 768], P(('grp', 'loc'))
- grad_w_down: bfloat16 [128, 768, 2048], P(('grp', 'loc'))
The draws below stay inside these ranges and needn't reach their ends.
Inputs may be any that keep to these rules, and one draw needn't show every extreme that they name: `expert_ids`: each token names 8 different experts. Among the 128 tokens of one device, no expert is named by more than 9 of them, and in every draw some expert is named by exactly 9 of one device's tokens.
All inputs are finite; a program needn't handle non-finite values.
Results may differ from the reference program's by a relative error of at most 0.0058.
Values may be sent and summed in bfloat16 or wider, within the bound.
No kernel may reach another device: no remote copies, remote signals or barrier semaphores. Data moves between devices by JAX's collectives and lax.ppermute only.
A program may use at most 128 MiB of HBM per device.

```python
import math
import jax
import jax.numpy as jnp
import numpy as np
from jax import lax

D = 2048
FF = 768
TOPK = 8
T_DEV = 128
EXPERTS = 128
CAP = 9
TOKENS = 16384
N_GRP = 16
N_LOC = 8


def shard_levels(stream_key, extent, split, least, top_value):
    factor_of, own = 1.0, jax.random.fold_in(stream_key, 6)
    for dim, blocks in split:
        heights = jnp.exp(jax.random.uniform(jax.random.fold_in(own, dim), (blocks,), jnp.float32, least / len(split), top_value / len(split)))
        factor_of = factor_of * jnp.repeat(heights, extent[dim] // blocks).reshape([-1 if axis == dim else 1 for axis in range(len(extent))])
    return factor_of


def routed_block(rng, own, number, rows, count, top, most, skew):
    sequence = jax.random.permutation(rng, count)
    packed, ordinary = load_shares(count, rows * top, most, skew, True), load_shares(count, rows * top, most, skew, False)
    places = jnp.arange(count)

    def named(sizes, rotation):
        used = int((sizes > 0).sum())
        fixed = max(1, used // 4)
        passed = fixed + (places - fixed + rotation * (used - fixed)) % max(1, count - fixed)
        return jnp.zeros((count,), jnp.int32).at[sequence[jnp.where(places < fixed, places, passed)]].set(jnp.asarray(sizes, jnp.int32))

    sizes = jnp.where(number % 4 == 0, named(packed, number // 4), named(ordinary, number - number // 4 - 1))
    mixed = jax.random.permutation(jax.random.fold_in(own, 3), count)
    giver, sink = mixed[0:count // 2 * 2:2], mixed[1:count // 2 * 2:2]
    room = jnp.minimum(sizes[giver] - 1, most - sizes[sink]) // 2
    room = jnp.where((giver == sequence[0]) | (sink == sequence[0]) | (sizes[sink] == 0), 0, jnp.maximum(room, 0))
    passed = jax.random.randint(jax.random.fold_in(own, 4), (count // 2,), 0, 1 << 20) % (room + 1)
    sizes = sizes.at[giver].add(-passed).at[sink].add(passed)
    members = jnp.searchsorted(jnp.cumsum(sizes), jnp.arange(rows * top), side="right").astype(jnp.int32)
    listing = members.reshape(top, rows).T
    listing = listing[jax.random.permutation(jax.random.fold_in(own, 1), rows)]
    rotation = jax.random.randint(jax.random.fold_in(own, 2), (rows, 1), 0, top)
    return jnp.take_along_axis(listing, (jnp.arange(top)[None, :] + rotation) % top, axis=1)


def load_shares(amount, total, reach, lean, full):
    portions = [(1 << 20) // math.isqrt(rank ** lean) + 1 for rank in range(1, amount + 1)]
    largest = reach if full else min(reach, max(-(-total // amount), total * portions[0] // sum(portions)))
    least = 1 if total - largest >= amount - 1 else 0
    counts, rest = [largest] + [least] * (amount - 1), total - largest - least * (amount - 1)
    while rest > 0:
        free = [i for i in range(1, amount) if counts[i] < largest] or [i for i in range(1, amount) if counts[i] < reach]
        mass, remaining = sum([portions[i] for i in free]), rest
        for i in free:
            more = min(reach - counts[i], max(1, remaining * portions[i] // mass), rest)
            counts[i] = counts[i] + more
            rest = rest - more
    return np.array(counts)


def bell_draw(stream_key, shape, scale, bound, shards=(), kind=jnp.bfloat16):
    values = scale * jax.random.normal(stream_key, shape, jnp.float32)
    if shards:
        values = values * shard_levels(stream_key, shape, shards, -0.22, 0.18)
    return jnp.clip(values, -bound, bound).astype(kind)


def setup_inputs(seed: int = 0) -> dict:
    arg_keys = jax.random.split(jax.random.key(seed), 8)
    acts = bell_draw(arg_keys[0], (TOKENS, D), 1.0, 6.0, ((0, 128),))
    out_grad = bell_draw(arg_keys[1], (TOKENS, D), 1.0, 6.0, ((0, 128),))
    expert_ids_keys = jax.random.split(jax.random.fold_in(arg_keys[2], 1), TOKENS // T_DEV)
    expert_ids_turns = jax.random.permutation(jax.random.fold_in(arg_keys[2], 3), TOKENS // T_DEV)
    expert_ids = jax.vmap(lambda own, number: routed_block(jax.random.fold_in(arg_keys[2], 2), own, number, T_DEV, EXPERTS, TOPK, CAP, 2))(expert_ids_keys, expert_ids_turns).reshape((TOKENS, TOPK))
    gate_vals = jnp.clip(jnp.exp(math.log(0.5) - 2.306499 * jax.random.uniform(arg_keys[3], (TOKENS, TOPK), jnp.float32) ** shard_levels(arg_keys[3], (TOKENS, TOPK), ((0, 128),), -0.2, 0.2)), 0.049804688, 0.5).astype(jnp.bfloat16)
    w_gate = bell_draw(arg_keys[4], (EXPERTS, D, FF), D ** -0.5, 0.125, ((0, 128),))
    w_up = bell_draw(arg_keys[5], (EXPERTS, D, FF), D ** -0.5, 0.125, ((0, 128),))
    w_down = bell_draw(arg_keys[6], (EXPERTS, FF, D), FF ** -0.5, 0.21875, ((0, 128),))
    return {"acts": acts, "out_grad": out_grad, "expert_ids": expert_ids, "gate_vals": gate_vals, "w_gate": w_gate, "w_up": w_up, "w_down": w_down}


def contract(left, right, left_dim, right_dim):
    return lax.dot_general(left, right, (((left_dim,), (right_dim,)), ((), ())), preferred_element_type=jnp.float32)


def expert_grads(rows_in, rows_grad, rows_gate, wg_one, wu_one, wd_one):
    gate_pre = jnp.dot(rows_in, wg_one, preferred_element_type=jnp.float32)
    up_proj = jnp.dot(rows_in, wu_one, preferred_element_type=jnp.float32)
    sigmoid_gate = jax.nn.sigmoid(gate_pre)
    activated = gate_pre * sigmoid_gate
    hidden = activated * up_proj
    dh_raw = contract(rows_grad, wd_one, 1, 1)
    gate_grad = jnp.sum(hidden * dh_raw, axis=1).astype(jnp.bfloat16)
    weight_col = rows_gate.astype(jnp.float32)[:, None]
    scaled_hidden = (weight_col * hidden).astype(jnp.bfloat16)
    down_grad = contract(scaled_hidden, rows_grad, 0, 0).astype(jnp.bfloat16)
    hidden_grad = weight_col * dh_raw
    pre_grad = (hidden_grad * up_proj * sigmoid_gate * (1.0 + gate_pre * (1.0 - sigmoid_gate))).astype(jnp.bfloat16)
    up_grad = (hidden_grad * activated).astype(jnp.bfloat16)
    wg_grad = contract(rows_in, pre_grad, 0, 0).astype(jnp.bfloat16)
    wu_grad = contract(rows_in, up_grad, 0, 0).astype(jnp.bfloat16)
    input_grad = (contract(pre_grad, wg_one, 1, 1) + contract(up_grad, wu_one, 1, 1)).astype(jnp.bfloat16)
    return input_grad, gate_grad, wg_grad, wu_grad, down_grad


def device_sources(dev_ids):
    flat_ids = dev_ids.reshape(-1)
    one_hot = (flat_ids[:, None] == jnp.arange(EXPERTS, dtype=jnp.int32)[None, :]).astype(jnp.int32)
    before = jnp.cumsum(one_hot, axis=0) - one_hot
    rank_in = jnp.sum(before * one_hot, axis=1)
    slot_of = flat_ids * CAP + rank_in
    entries = T_DEV * TOPK
    return jnp.full((EXPERTS * CAP,), entries, jnp.int32).at[slot_of].set(jnp.arange(entries, dtype=jnp.int32))


def reference(acts, out_grad, expert_ids, gate_vals, w_gate, w_up, w_down):
    devices = N_GRP * N_LOC
    entries = T_DEV * TOPK
    sources = jax.vmap(device_sources)(expert_ids.reshape(devices, T_DEV, TOPK))
    padded_acts = jnp.concatenate([acts, jnp.zeros((1, D), acts.dtype)], axis=0)
    padded_grad = jnp.concatenate([out_grad, jnp.zeros((1, D), out_grad.dtype)], axis=0)
    padded_gate = jnp.concatenate([gate_vals.reshape(-1), jnp.zeros((1,), gate_vals.dtype)], axis=0)
    dev_base = jnp.arange(devices, dtype=jnp.int32)[:, None]

    def one_expert(carry, expert):
        acc_rows, acc_gate = carry
        cols = lax.dynamic_slice_in_dim(sources, expert * CAP, CAP, 1)
        valid = cols < entries
        row_index = jnp.where(valid, dev_base * T_DEV + cols // TOPK, TOKENS).reshape(-1).astype(jnp.int32)
        gate_index = jnp.where(valid, dev_base * entries + cols, TOKENS * TOPK).reshape(-1).astype(jnp.int32)
        input_grad, gate_grad, wg_grad, wu_grad, down_grad = expert_grads(
            padded_acts[row_index], padded_grad[row_index], padded_gate[gate_index],
            w_gate[expert], w_up[expert], w_down[expert])
        acc_rows = acc_rows.at[row_index].add(input_grad.astype(jnp.float32))
        acc_gate = acc_gate.at[gate_index].set(gate_grad.astype(jnp.float32))
        return (acc_rows, acc_gate), (wg_grad, wu_grad, down_grad)

    start = (jnp.zeros((TOKENS + 1, D), jnp.float32), jnp.zeros((TOKENS * TOPK + 1,), jnp.float32))
    (acc_rows, acc_gate), (grad_w_gate, grad_w_up, grad_w_down) = lax.scan(
        one_expert, start, jnp.arange(EXPERTS, dtype=jnp.int32))
    grad_acts = acc_rows[:TOKENS].astype(jnp.bfloat16)
    grad_gates = acc_gate[:TOKENS * TOPK].reshape(TOKENS, TOPK).astype(jnp.bfloat16)
    return grad_acts, grad_gates, grad_w_gate, grad_w_up, grad_w_down
```

```python
import functools

import jax
import jax.numpy as jnp
from jax import lax
from jax.experimental import pallas as pl
from jax.experimental.pallas import tpu as pltpu
from jax.sharding import PartitionSpec as P

AXES = ("grp", "loc")
BF = jnp.bfloat16
F32 = jnp.float32
E = 128
T = 128
R8 = 1024
ROWS = 1152
D = 2048
FF = 768
LANE = 128
SUB = 8
FOLD = D // SUB
WIDE = D + FOLD
WIDE_G = WIDE + LANE
TN = 512
PIECES = TN // FOLD


def dot(a, b, ca=1, cb=0):
    return lax.dot_general(a, b, (((ca,), (cb,)), ((), ())), preferred_element_type=F32)


def nine_rows(i):
    return pl.ds(i, E, stride=SUB)


def fold_in(fold, i, value):
    for h in range(FOLD // LANE):
        fold[h, nine_rows(i), :] = value[:, h * LANE : (h + 1) * LANE]


def fold_out(fold, i):
    return jnp.concatenate(
        [fold[h, nine_rows(i), :] for h in range(FOLD // LANE)], axis=1
    )


def params(steps=1, limit=None):
    return pltpu.CompilerParams(
        dimension_semantics=("arbitrary",) * steps, vmem_limit_bytes=limit
    )


def cost(flops, bytes_accessed):
    return pl.CostEstimate(
        flops=int(flops), bytes_accessed=int(bytes_accessed), transcendentals=0
    )


def pack_acts_kernel(ids_ref, gates_ref, x_ref, out_ref, sel_ref, sel9_ref, fold, gate_blk):
    j = pl.program_id(0)

    @pl.when(j == 0)
    def _():
        expert = lax.broadcasted_iota(jnp.int32, (E, T), 0)
        member = jnp.zeros((E, T), F32)
        gate = jnp.zeros((E, T), F32)
        for k in range(8):
            hit = ids_ref[k : k + 1, :] == expert
            member = jnp.where(hit, 1.0, member)
            gate = jnp.where(hit, gates_ref[k : k + 1, :].astype(F32), gate)
        earlier = (
            lax.broadcasted_iota(jnp.int32, (T, T), 0)
            < lax.broadcasted_iota(jnp.int32, (T, T), 1)
        ).astype(F32)
        rank = dot(member.astype(BF), earlier.astype(BF))
        rank = jnp.where(member > 0.0, rank, -1.0)
        slot = lax.broadcasted_iota(jnp.int32, (E, SUB, T), 1).astype(F32)
        sel = jnp.where(rank[:, None, :] == slot, 1.0, 0.0)
        sel9 = jnp.where(rank == float(SUB), 1.0, 0.0)
        sel_gate = (sel * gate[:, None, :]).reshape(R8, T)
        sel_ref[...] = sel.reshape(R8, T).astype(BF)
        sel9_ref[...] = sel9.astype(BF)
        ones = jnp.ones((T, LANE), BF)
        own = dot(sel_gate.astype(BF), ones)
        ninth = dot((sel9 * gate).astype(BF), ones)
        ninth = jnp.broadcast_to(ninth[:, None, :], (E, SUB, LANE)).reshape(R8, LANE)
        lane = lax.broadcasted_iota(jnp.int32, (R8, LANE), 1)
        gate_blk[...] = jnp.where(lane == 1, ninth, own).astype(BF)

    @pl.when(j < D // TN)
    def _():
        x = x_ref[...]
        out_ref[...] = dot(sel_ref[...], x).astype(BF)
        nine = dot(sel9_ref[...], x)
        for p in range(PIECES):
            fold_in(fold, j * PIECES + p, nine[:, p * FOLD : (p + 1) * FOLD])

    @pl.when(j == D // TN)
    def _():
        for h in range(FOLD // LANE):
            out_ref[:, h * LANE : (h + 1) * LANE] = fold[h].astype(BF)
        out_ref[:, FOLD : FOLD + LANE] = gate_blk[...]


def pack_acts(ids_t, gates_t, acts):
    last = D // TN - 1
    return pl.pallas_call(
        pack_acts_kernel,
        grid=(D // TN + 1,),
        in_specs=[
            pl.BlockSpec((8, T), lambda j: (0, 0)),
            pl.BlockSpec((8, T), lambda j: (0, 0)),
            pl.BlockSpec((T, TN), lambda j: (0, jnp.minimum(j, last))),
        ],
        out_specs=[
            pl.BlockSpec((R8, TN), lambda j: (0, j)),
            pl.BlockSpec((R8, T), lambda j: (0, 0)),
            pl.BlockSpec((E, T), lambda j: (0, 0)),
        ],
        out_shape=[
            jax.ShapeDtypeStruct((R8, WIDE_G), BF),
            jax.ShapeDtypeStruct((R8, T), BF),
            jax.ShapeDtypeStruct((E, T), BF),
        ],
        scratch_shapes=[
            pltpu.VMEM((FOLD // LANE, R8, LANE), F32),
            pltpu.VMEM((R8, LANE), BF),
        ],
        compiler_params=params(),
        cost_estimate=cost(2 * ROWS * T * D, 2 * (R8 * WIDE_G + T * D)),
        name="pack_acts",
    )(ids_t, gates_t, acts)


def pack_grad_kernel(sel_ref, sel9_ref, x_ref, out_ref, fold):
    j = pl.program_id(0)

    @pl.when(j < D // TN)
    def _():
        x = x_ref[...]
        out_ref[...] = dot(sel_ref[...], x).astype(BF)
        nine = dot(sel9_ref[...], x)
        for p in range(PIECES):
            fold_in(fold, j * PIECES + p, nine[:, p * FOLD : (p + 1) * FOLD])

    @pl.when(j == D // TN)
    def _():
        for h in range(FOLD // LANE):
            out_ref[:, h * LANE : (h + 1) * LANE] = fold[h].astype(BF)


def pack_grad(sel, sel9, grad):
    last = D // TN - 1
    return pl.pallas_call(
        pack_grad_kernel,
        grid=(D // TN + 1,),
        in_specs=[
            pl.BlockSpec((R8, T), lambda j: (0, 0)),
            pl.BlockSpec((E, T), lambda j: (0, 0)),
            pl.BlockSpec((T, TN), lambda j: (0, jnp.minimum(j, last))),
        ],
        out_specs=pl.BlockSpec((R8, TN), lambda j: (0, j)),
        out_shape=jax.ShapeDtypeStruct((R8, WIDE), BF),
        scratch_shapes=[pltpu.VMEM((FOLD // LANE, R8, LANE), F32)],
        compiler_params=params(),
        cost_estimate=cost(2 * ROWS * T * D, 2 * (R8 * WIDE + T * D)),
        name="pack_grad",
    )(sel, sel9, grad)


TF = 256
MB = 384


def unfold(fold, y_ref, rows_ref):
    rows_ref[0:R8, :] = y_ref[:, 0:D]
    for h in range(FOLD // LANE):
        fold[h] = y_ref[:, D + h * LANE : D + (h + 1) * LANE].astype(F32)
    for i in range(SUB):
        rows_ref[R8:ROWS, i * FOLD : (i + 1) * FOLD] = fold_out(fold, i).astype(BF)


def acts_kernel(y_ref, wg_ref, wu_ref, rows_ref, a_ref, b_ref, hid_ref, hw_ref, fold, gcol):
    i = pl.program_id(0)

    @pl.when(i == 0)
    def _():
        unfold(fold, y_ref, rows_ref)
        fold[0] = y_ref[:, WIDE:WIDE_G].astype(F32)
        gcol[0:R8, :] = jnp.broadcast_to(fold[0, :, 0:1], (R8, LANE))
        ninth = fold[0, nine_rows(0), :]
        gcol[R8:ROWS, :] = jnp.broadcast_to(ninth[:, 1:2], (E, LANE))

    for m in range(ROWS // MB):
        rows = pl.ds(m * MB, MB)
        x = rows_ref[rows, :]
        pre = dot(x, wg_ref[...])
        up = dot(x, wu_ref[...])
        gate = jnp.concatenate([gcol[rows, :]] * (TF // LANE), axis=1)
        s = jax.nn.sigmoid(pre)
        act = pre * s
        hid = act * up
        hid_ref[rows, :] = hid
        hw_ref[rows, :] = (gate * hid).astype(BF)
        a_ref[rows, :] = gate * (up * s * (1.0 + pre * (1.0 - s)))
        b_ref[rows, :] = gate * act


def acts_side(y, wg, wu):
    tile = lambda i: (0, i)
    return pl.pallas_call(
        acts_kernel,
        grid=(FF // TF,),
        in_specs=[
            pl.BlockSpec((R8, WIDE_G), lambda i: (0, 0), pipeline_mode=pl.Buffered(1)),
            pl.BlockSpec((D, TF), tile),
            pl.BlockSpec((D, TF), tile),
        ],
        out_specs=[
            pl.BlockSpec((ROWS, D), lambda i: (0, 0), pipeline_mode=pl.Buffered(1)),
            pl.BlockSpec((ROWS, TF), tile),
            pl.BlockSpec((ROWS, TF), tile),
            pl.BlockSpec((ROWS, TF), tile),
            pl.BlockSpec((ROWS, TF), tile),
        ],
        out_shape=[
            jax.ShapeDtypeStruct((ROWS, D), BF),
            jax.ShapeDtypeStruct((ROWS, FF), F32),
            jax.ShapeDtypeStruct((ROWS, FF), F32),
            jax.ShapeDtypeStruct((ROWS, FF), F32),
            jax.ShapeDtypeStruct((ROWS, FF), BF),
        ],
        scratch_shapes=[
            pltpu.VMEM((FOLD // LANE, R8, LANE), F32),
            pltpu.VMEM((ROWS, LANE), F32),
        ],
        compiler_params=params(),
        cost_estimate=cost(4 * ROWS * D * FF, 30e6),
        name="acts_side",
    )(y, wg, wu)


N1 = FF // TF
N2 = D // TN


def grads_kernel(
    y_ref, wd_ref, a_ref, b_ref, hid_ref, wg_ref, wu_ref,
    out_ref, rows_ref, dpre_ref, dup_ref, fold, gsum,
):
    i = pl.program_id(0)

    @pl.when(i == 0)
    def _():
        unfold(fold, y_ref, rows_ref)
        gsum[...] = jnp.zeros_like(gsum)

    @pl.when(i < N1)
    def _():
        cols = pl.ds(pl.multiple_of(jnp.minimum(i, N1 - 1) * TF, TF), TF)
        for m in range(ROWS // MB):
            rows = pl.ds(m * MB, MB)
            dh = dot(rows_ref[rows, :], wd_ref[...], 1, 1)
            gg = hid_ref[rows, :] * dh
            gsum[rows, :] += gg[:, 0:LANE] + gg[:, LANE:TF]
            dpre_ref[rows, cols] = (dh * a_ref[rows, :]).astype(BF)
            dup_ref[rows, cols] = (dh * b_ref[rows, :]).astype(BF)

    @pl.when((i >= N1) & (i < N1 + N2))
    def _():
        for m in range(ROWS // MB):
            rows = pl.ds(m * MB, MB)
            dx = dot(dpre_ref[rows, :], wg_ref[...], 1, 1)
            dx = dx + dot(dup_ref[rows, :], wu_ref[...], 1, 1)
            keep = min(MB, R8 - m * MB)
            out_ref[m * MB : m * MB + keep, :] = dx[0:keep].astype(BF)
            if keep < MB:
                for p in range(PIECES):
                    fold_in(
                        fold,
                        (i - N1) * PIECES + p,
                        dx[keep:MB, p * FOLD : (p + 1) * FOLD],
                    )

    @pl.when(i == N1 + N2)
    def _():
        for h in range(FOLD // LANE):
            out_ref[:, h * LANE : (h + 1) * LANE] = fold[h].astype(BF)
        total = jnp.sum(gsum[...], axis=1, keepdims=True)
        ninth = jnp.broadcast_to(total[R8:ROWS], (E, LANE))
        for s in range(SUB):
            fold[0, nine_rows(s), :] = ninth
        lane = lax.broadcasted_iota(jnp.int32, (R8, LANE), 1)
        own = jnp.broadcast_to(total[0:R8], (R8, LANE))
        out_ref[:, FOLD : FOLD + LANE] = jnp.where(lane == 1, fold[0], own).astype(BF)


def grads_side(y, wd, a, b, hid, wg, wu):
    first = lambda i: (0, jnp.minimum(i, N1 - 1))
    second = lambda i: (jnp.clip(i - N1, 0, N2 - 1), 0)
    whole = lambda i: (0, 0)
    one = pl.Buffered(1)
    return pl.pallas_call(
        grads_kernel,
        grid=(N1 + N2 + 1,),
        in_specs=[
            pl.BlockSpec((R8, WIDE), whole, pipeline_mode=one),
            pl.BlockSpec((TF, D), lambda i: (jnp.minimum(i, N1 - 1), 0)),
            pl.BlockSpec((ROWS, TF), first),
            pl.BlockSpec((ROWS, TF), first),
            pl.BlockSpec((ROWS, TF), first),
            pl.BlockSpec((TN, FF), second),
            pl.BlockSpec((TN, FF), second),
        ],
        out_specs=[
            pl.BlockSpec((R8, TN), lambda i: (0, jnp.maximum(i - N1, 0))),
            pl.BlockSpec((ROWS, D), whole, pipeline_mode=one),
            pl.BlockSpec((ROWS, FF), whole, pipeline_mode=one),
            pl.BlockSpec((ROWS, FF), whole, pipeline_mode=one),
        ],
        out_shape=[
            jax.ShapeDtypeStruct((R8, WIDE_G), BF),
            jax.ShapeDtypeStruct((ROWS, D), BF),
            jax.ShapeDtypeStruct((ROWS, FF), BF),
            jax.ShapeDtypeStruct((ROWS, FF), BF),
        ],
        scratch_shapes=[
            pltpu.VMEM((FOLD // LANE, R8, LANE), F32),
            pltpu.VMEM((ROWS, LANE), F32),
        ],
        compiler_params=params(),
        cost_estimate=cost(6 * ROWS * D * FF, 36e6),
        name="grads_side",
    )(y, wd, a, b, hid, wg, wu)


def combine_kernel(ids_ref, sel_ref, sel9_ref, y_ref, y9_ref, yg_ref, out_ref, gg_ref, fold):
    j = pl.program_id(0)

    @pl.when(j == 0)
    def _():
        fold[0] = yg_ref[...].astype(F32)
        own = jnp.broadcast_to(fold[0, :, 0:1], (R8, T))
        ninth = jnp.broadcast_to(fold[0, nine_rows(0), :][:, 1:2], (E, T))
        sel = sel_ref[...].astype(F32)
        picked = jnp.where(sel > 0.0, own, 0.0).reshape(E, SUB, T)
        table = jnp.sum(picked, axis=1)
        table = table + jnp.where(sel9_ref[...].astype(F32) > 0.0, ninth, 0.0)
        expert = lax.broadcasted_iota(jnp.int32, (E, T), 0)
        for k in range(8):
            hit = ids_ref[k : k + 1, :] == expert
            gg_ref[k : k + 1, :] = jnp.sum(
                jnp.where(hit, table, 0.0), axis=0, keepdims=True
            )
        for h in range(FOLD // LANE):
            fold[h] = y9_ref[:, h * LANE : (h + 1) * LANE].astype(F32)

    acc = dot(sel_ref[...], y_ref[...], 0, 0)
    nine = jnp.concatenate(
        [fold_out(fold, j * PIECES + p) for p in range(PIECES)], axis=1
    ).astype(BF)
    out_ref[...] = (acc + dot(sel9_ref[...], nine, 0, 0)).astype(BF)


def combine(ids_t, sel, sel9, y):
    whole = lambda j: (0, 0)
    return pl.pallas_call(
        combine_kernel,
        grid=(D // TN,),
        in_specs=[
            pl.BlockSpec((8, T), whole),
            pl.BlockSpec((R8, T), whole),
            pl.BlockSpec((E, T), whole),
            pl.BlockSpec((R8, TN), lambda j: (0, j)),
            pl.BlockSpec((R8, FOLD), lambda j: (0, D // FOLD)),
            pl.BlockSpec((R8, LANE), lambda j: (0, WIDE // LANE)),
        ],
        out_specs=[
            pl.BlockSpec((T, TN), lambda j: (0, j)),
            pl.BlockSpec((8, T), whole),
        ],
        out_shape=[
            jax.ShapeDtypeStruct((T, D), BF),
            jax.ShapeDtypeStruct((8, T), F32),
        ],
        scratch_shapes=[pltpu.VMEM((FOLD // LANE, R8, LANE), F32)],
        compiler_params=params(),
        cost_estimate=cost(2 * ROWS * T * D, 2 * (R8 * WIDE_G + T * D)),
        name="combine",
    )(ids_t, sel, sel9, y, y, y)


def exchange(x):
    width = x.shape[1]
    y = lax.all_to_all(
        x.reshape(E, SUB, width), AXES, split_axis=0, concat_axis=0, tiled=True
    )
    return y.reshape(R8, width)


def body(acts, out_grad, expert_ids, gate_vals, w_gate, w_up, w_down):
    ids_t = expert_ids.T
    gates_t = gate_vals.T
    wg, wu, wd = w_gate[0], w_up[0], w_down[0]
    send_acts, sel, sel9 = pack_acts(ids_t, gates_t, acts)
    got_acts = exchange(send_acts)
    send_grad = pack_grad(sel, sel9, out_grad)
    got_grad = exchange(send_grad)
    rows_in, coef_pre, coef_up, hidden, scaled = acts_side(got_acts, wg, wu)
    back, rows_grad, dpre, dup = grads_side(
        got_grad, wd, coef_pre, coef_up, hidden, wg, wu
    )
    got_back = exchange(back)
    wg_grad = dot(rows_in, dpre, 0, 0).astype(BF)
    wu_grad = dot(rows_in, dup, 0, 0).astype(BF)
    wd_grad = dot(scaled, rows_grad, 0, 0).astype(BF)
    grad_acts, gate_grad_t = combine(ids_t, sel, sel9, got_back)
    return (
        grad_acts,
        gate_grad_t.astype(BF).T,
        wg_grad[None],
        wu_grad[None],
        wd_grad[None],
    )


def solution(mesh):
    rows = P(AXES, None)
    mats = P(AXES, None, None)
    return jax.shard_map(
        body,
        mesh=mesh,
        in_specs=(rows, rows, rows, rows, mats, mats, mats),
        out_specs=(rows, rows, mats, mats, mats),
        check_vma=False,
    )
```

```python
import functools

import jax
import jax.numpy as jnp
from jax import lax
from jax.experimental import pallas as pl
from jax.experimental.pallas import tpu as pltpu
from jax.sharding import PartitionSpec as P

AXES = ("grp", "loc")
BF = jnp.bfloat16
F32 = jnp.float32
E = 128
T = 128
K = 8
D = 2048
FF = 768
LANE = 128
SUB = 8
R8 = E * SUB
HALF = D // 2
HL = HALF // LANE
FOLD = D // SUB
FL = FOLD // LANE
GROUP = 4 * E
ROWS_A = GROUP + E
SEND_A = 2 * HALF + 2 * FOLD
SEND_B = 2 * HALF
BACK_A = HALF + FOLD
BACK_B = HALF + LANE
TN = 512
TF = 256
N1 = FF // TF
N2 = D // TN


def dot(a, b, ca=1, cb=0):
    return lax.dot_general(a, b, (((ca,), (cb,)), ((), ())), preferred_element_type=F32)


def cost(flops, bytes_accessed):
    return pl.CostEstimate(
        flops=int(flops), bytes_accessed=int(bytes_accessed), transcendentals=0
    )


ONE_DIM = pltpu.CompilerParams(dimension_semantics=("arbitrary",))
SINGLE = pl.Buffered(1)


def lanes(i):
    return slice(i * LANE, (i + 1) * LANE)


def halves(x, start, width):
    return jnp.concatenate(
        [x[:, start : start + width], x[:, HALF + start : HALF + start + width]], axis=0
    )


def pair_select(rank, weight, base):
    sub = lax.broadcasted_iota(jnp.int32, (E, SUB, T), 1)
    slot = (base + sub // 2).astype(F32)
    hit = jnp.where(rank[:, None, :] == slot, weight, 0.0)
    even = (sub % 2) == 0
    left = jnp.where(even, hit, 0.0).reshape(R8, T)
    right = jnp.where(even, 0.0, hit).reshape(R8, T)
    return jnp.concatenate([left, right], axis=1).astype(BF)


def pack_a_kernel(
    ids_hbm, gates_hbm, x_hbm, g_hbm, out_hbm, sel_hbm, sel9_hbm, rank_hbm, gate_hbm,
    ids_ref, gates_ref, x_ref, g_ref, sel_ref, sel9_ref, rank_ref, gate_ref,
    selg, fold, out, in_sems, out_sems,
):
    loads = [
        pltpu.make_async_copy(source, target, in_sems.at[n])
        for n, (source, target) in enumerate(
            (
                (ids_hbm, ids_ref),
                (gates_hbm, gates_ref),
                (x_hbm, x_ref),
                (g_hbm, g_ref),
            )
        )
    ]
    for load in loads:
        load.start()
    stores = []

    def send(source, target):
        store = pltpu.make_async_copy(source, target, out_sems.at[len(stores)])
        store.start()
        stores.append(store)

    def send_piece(piece):
        cols = pl.ds(piece * TN, TN)
        send(out.at[:, cols], out_hbm.at[:, cols])

    loads[0].wait()
    loads[1].wait()
    expert = lax.broadcasted_iota(jnp.int32, (E, T), 0)
    member = jnp.zeros((E, T), F32)
    gate = jnp.zeros((E, T), F32)
    for k in range(K):
        hit = ids_ref[k : k + 1, :] == expert
        member = jnp.where(hit, 1.0, member)
        gate = jnp.where(hit, gates_ref[k : k + 1, :].astype(F32), gate)
    earlier = (
        lax.broadcasted_iota(jnp.int32, (T, T), 0)
        < lax.broadcasted_iota(jnp.int32, (T, T), 1)
    ).astype(F32)
    rank = dot(member.astype(BF), earlier.astype(BF))
    rank = jnp.where(member > 0.0, rank, -1.0)
    rank_ref[...] = rank
    gate_ref[...] = gate
    sel9 = jnp.where(rank == float(SUB), 1.0, 0.0)
    sel9_ref[...] = sel9.astype(BF)
    sel9g = (sel9 * gate).astype(BF)
    sel_ref[...] = pair_select(rank, 1.0, 0)
    selg[...] = pair_select(rank, gate[:, None, :], 0)

    tiles = HALF // TN
    loads[2].wait()
    for c in range(tiles):
        out[:, c * TN : (c + 1) * TN] = dot(
            sel_ref[...], halves(x_ref, c * TN, TN)
        ).astype(BF)
        send_piece(c)
    loads[3].wait()
    for c in range(tiles):
        at = (tiles + 1 + c) * TN
        out[:, at : at + TN] = dot(selg[...], halves(g_ref, c * TN, TN)).astype(BF)
        send_piece(tiles + 1 + c)
    nine = dot(sel9_ref[...], x_ref[...])
    nine_g = dot(sel9g, g_ref[...])
    for i in range(SUB):
        rows = pl.ds(i, E, stride=SUB)
        for h in range(FL):
            at = i * FOLD + h * LANE
            fold[h, rows, :] = nine[:, at : at + LANE]
            fold[FL + h, rows, :] = nine_g[:, at : at + LANE]
    for h in range(2 * FL):
        at = HALF + h * LANE
        out[:, at : at + LANE] = fold[h].astype(BF)
    send_piece(tiles)
    send(sel_ref, sel_hbm)
    send(sel9_ref, sel9_hbm)
    send(rank_ref, rank_hbm)
    send(gate_ref, gate_hbm)
    for store in stores:
        store.wait()


def pack_a(ids_t, gates_t, acts, grad):
    return pl.pallas_call(
        pack_a_kernel,
        in_specs=[pl.BlockSpec(memory_space=pl.ANY)] * 4,
        out_specs=[pl.BlockSpec(memory_space=pl.ANY)] * 5,
        out_shape=[
            jax.ShapeDtypeStruct((R8, SEND_A), BF),
            jax.ShapeDtypeStruct((R8, 2 * T), BF),
            jax.ShapeDtypeStruct((E, T), BF),
            jax.ShapeDtypeStruct((E, T), F32),
            jax.ShapeDtypeStruct((E, T), F32),
        ],
        scratch_shapes=[
            pltpu.VMEM((K, T), jnp.int32),
            pltpu.VMEM((K, T), BF),
            pltpu.VMEM((T, D), BF),
            pltpu.VMEM((T, D), BF),
            pltpu.VMEM((R8, 2 * T), BF),
            pltpu.VMEM((E, T), BF),
            pltpu.VMEM((E, T), F32),
            pltpu.VMEM((E, T), F32),
            pltpu.VMEM((R8, 2 * T), BF),
            pltpu.VMEM((2 * FL, R8, LANE), F32),
            pltpu.VMEM((R8, SEND_A), BF),
            pltpu.SemaphoreType.DMA((4,)),
            pltpu.SemaphoreType.DMA((SEND_A // TN + 4,)),
        ],
        cost_estimate=cost(4 * R8 * T * D, 2 * R8 * SEND_A + 4 * T * D),
        name="pack_a",
    )(ids_t, gates_t, acts, grad)


def pack_b_kernel(rank_ref, gate_ref, x_ref, g_ref, out_ref, sel_t_ref, mix_ref, sel, selg):
    j = pl.program_id(0)
    tiles = HALF // TN

    @pl.when(j == 0)
    def _():
        rank = rank_ref[...]
        sel[...] = pair_select(rank, 1.0, 4)
        selg[...] = pair_select(rank, gate_ref[...][:, None, :], 4)
        sub = lax.broadcasted_iota(jnp.int32, (E, SUB, T), 1)
        slot = (sub // 2 + 4 * (sub % 2)).astype(F32)
        mix_ref[...] = jnp.where(rank[:, None, :] == slot, 1.0, 0.0).reshape(R8, T).astype(BF)

    @pl.when(j == 1)
    def _():
        sel_t_ref[...] = sel[...].T

    for c in range(tiles):

        @pl.when(j == c)
        def _():
            out_ref[...] = dot(sel[...], halves(x_ref, c * TN, TN)).astype(BF)

        @pl.when(j == tiles + c)
        def _():
            out_ref[...] = dot(selg[...], halves(g_ref, c * TN, TN)).astype(BF)


def pack_b(rank, gate, acts, grad):
    whole = lambda j: (0, 0)
    return pl.pallas_call(
        pack_b_kernel,
        grid=(SEND_B // TN,),
        in_specs=[
            pl.BlockSpec((E, T), whole),
            pl.BlockSpec((E, T), whole),
            pl.BlockSpec((T, D), whole),
            pl.BlockSpec((T, D), whole),
        ],
        out_specs=[
            pl.BlockSpec((R8, TN), lambda j: (0, j)),
            pl.BlockSpec((2 * T, R8), whole),
            pl.BlockSpec((R8, T), whole),
        ],
        out_shape=[
            jax.ShapeDtypeStruct((R8, SEND_B), BF),
            jax.ShapeDtypeStruct((2 * T, R8), BF),
            jax.ShapeDtypeStruct((R8, T), BF),
        ],
        scratch_shapes=[pltpu.VMEM((R8, 2 * T), BF), pltpu.VMEM((R8, 2 * T), BF)],
        compiler_params=ONE_DIM,
        cost_estimate=cost(4 * R8 * T * D, 2 * R8 * SEND_B + 4 * T * D),
        name="pack_b",
    )(rank, gate, acts, grad)


def expert_kernel(
    nine, y_ref, wg_ref, wu_ref, wd_ref, wg2_ref, wu2_ref, *rest
):
    if nine:
        out_ref, x_ref, g_ref, dpre_ref, dup_ref, hid_ref, tot_ref, fold, gsum = rest
    else:
        tot_ref, out_ref, x_ref, g_ref, dpre_ref, dup_ref, hid_ref, fold, gsum = rest
    i = pl.program_id(0)
    rows_all = GROUP + (E if nine else 0)
    step = rows_all // 2
    after = HALF + (2 * FOLD if nine else 0)

    def unfold(base, base9, rows_ref):
        for c in range(HL):
            at = base + c * LANE
            fold[c] = y_ref[:, at : at + LANE].astype(F32)
            for h in range(2):
                to = h * HALF + c * LANE
                rows_ref[0:GROUP, to : to + LANE] = fold[
                    c, pl.ds(h, GROUP, stride=2), :
                ].astype(BF)
        if nine:
            for h in range(FL):
                at = base9 + h * LANE
                fold[h] = y_ref[:, at : at + LANE].astype(F32)
            for s in range(SUB):
                for h in range(FL):
                    to = s * FOLD + h * LANE
                    rows_ref[GROUP:rows_all, to : to + LANE] = fold[
                        h, pl.ds(s, E, stride=SUB), :
                    ].astype(BF)

    @pl.when(i == 0)
    def _():
        unfold(0, HALF, x_ref)
        unfold(after, HALF + FOLD, g_ref)
        gsum[...] = jnp.zeros_like(gsum)

    @pl.when(i < N1)
    def _():
        cols = pl.ds(pl.multiple_of(jnp.minimum(i, N1 - 1) * TF, TF), TF)
        for m in range(2):
            rows = pl.ds(m * step, step)
            x = x_ref[rows, :]
            pre = dot(x, wg_ref[...])
            up = dot(x, wu_ref[...])
            dh = dot(g_ref[rows, :], wd_ref[...], 1, 1)
            s = jax.nn.sigmoid(pre)
            act = pre * s
            hid = act * up
            part = hid * dh
            gsum[rows, :] += part[:, 0:LANE] + part[:, LANE:TF]
            hid_ref[rows, cols] = hid.astype(BF)
            dup_ref[rows, cols] = (dh * act).astype(BF)
            dpre_ref[rows, cols] = (dh * up * s * (1.0 + pre * (1.0 - s))).astype(BF)

    @pl.when((i >= N1) & (i < N1 + N2))
    def _():
        j = i - N1
        half = j // 2
        for m in range(2):
            rows = pl.ds(m * step, step)
            dx = dot(dpre_ref[rows, :], wg2_ref[...], 1, 1)
            dx = dx + dot(dup_ref[rows, :], wu2_ref[...], 1, 1)
            keep = min(step, GROUP - m * step)
            for q in range(TN // LANE):
                fold[
                    (j % 2) * (TN // LANE) + q,
                    pl.ds(2 * m * step + half, keep, stride=2),
                    :,
                ] = dx[0:keep, lanes(q)]
            if keep < step:
                for q in range(TN // LANE):
                    fold[HL + q % FL, pl.ds(j * (TN // FOLD) + q // FL, E, stride=SUB), :] = dx[
                        keep:step, lanes(q)
                    ]

    @pl.when(i == N1 + N2)
    def _():
        for c in range(HL + (FL if nine else 0)):
            out_ref[:, lanes(c)] = fold[c].astype(BF)
        total = jnp.sum(gsum[...], axis=1, keepdims=True)
        total = jnp.broadcast_to(total, (rows_all, LANE))
        if nine:
            tot_ref[...] = total
        else:
            fold[0, pl.ds(0, GROUP, stride=2), :] = tot_ref[0:GROUP, :]
            fold[0, pl.ds(1, GROUP, stride=2), :] = total
            for s in range(SUB):
                fold[1, pl.ds(s, E, stride=SUB), :] = tot_ref[GROUP:ROWS_A, :]
            lane = lax.broadcasted_iota(jnp.int32, (R8, LANE), 1)
            out_ref[:, lanes(HL)] = jnp.where(lane == 1, fold[1], fold[0]).astype(BF)


def expert_side(nine, y, wg, wu, wd, *totals):
    rows_all = GROUP + (E if nine else 0)
    send, back = (SEND_A, BACK_A) if nine else (SEND_B, BACK_B)
    first = lambda i: (0, jnp.minimum(i, N1 - 1))
    second = lambda i: (jnp.clip(i - N1, 0, N2 - 1), 0)
    whole = lambda i: (0, 0)
    return pl.pallas_call(
        functools.partial(expert_kernel, nine),
        grid=(N1 + N2 + 1,),
        in_specs=[
            pl.BlockSpec((R8, send), whole, pipeline_mode=SINGLE),
            pl.BlockSpec((D, TF), first),
            pl.BlockSpec((D, TF), first),
            pl.BlockSpec((TF, D), lambda i: (jnp.minimum(i, N1 - 1), 0)),
            pl.BlockSpec((TN, FF), second),
            pl.BlockSpec((TN, FF), second),
        ]
        + [pl.BlockSpec((ROWS_A, LANE), whole) for _ in totals],
        out_specs=[
            pl.BlockSpec((R8, back), whole, pipeline_mode=SINGLE),
            pl.BlockSpec((rows_all, D), whole, pipeline_mode=SINGLE),
            pl.BlockSpec((rows_all, D), whole, pipeline_mode=SINGLE),
            pl.BlockSpec((rows_all, FF), whole, pipeline_mode=SINGLE),
            pl.BlockSpec((rows_all, FF), whole, pipeline_mode=SINGLE),
            pl.BlockSpec((rows_all, FF), whole, pipeline_mode=SINGLE),
        ]
        + [pl.BlockSpec((ROWS_A, LANE), whole)] * nine,
        out_shape=[
            jax.ShapeDtypeStruct((R8, back), BF),
            jax.ShapeDtypeStruct((rows_all, D), BF),
            jax.ShapeDtypeStruct((rows_all, D), BF),
            jax.ShapeDtypeStruct((rows_all, FF), BF),
            jax.ShapeDtypeStruct((rows_all, FF), BF),
            jax.ShapeDtypeStruct((rows_all, FF), BF),
        ]
        + [jax.ShapeDtypeStruct((ROWS_A, LANE), F32)] * nine,
        scratch_shapes=[
            pltpu.VMEM((HL + FL, R8, LANE), F32),
            pltpu.VMEM((rows_all, LANE), F32),
        ],
        compiler_params=ONE_DIM,
        cost_estimate=cost(10 * rows_all * D * FF, 40e6),
        name="expert_a" if nine else "expert_b",
    )(y, wg, wu, wd, wg, wu, *totals)


def combine_a_kernel(sel_ref, sel9_ref, y_ref, y9_ref, out_ref, fold, nine):
    j = pl.program_id(0)

    @pl.when(j == 0)
    def _():
        for h in range(FL):
            fold[h] = y9_ref[:, lanes(h)].astype(F32)
        for s in range(SUB):
            for h in range(FL):
                at = s * FOLD + h * LANE
                nine[:, at : at + LANE] = fold[h, pl.ds(s, E, stride=SUB), :].astype(BF)

    acc = dot(sel_ref[...], y_ref[...], 0, 0)
    cols = pl.ds(pl.multiple_of(j * TN, TN), TN)
    cols2 = pl.ds(pl.multiple_of(HALF + j * TN, TN), TN)
    out_ref[0:T, :] = acc[0:T] + dot(sel9_ref[...], nine[:, cols], 0, 0)
    out_ref[T : 2 * T, :] = acc[T : 2 * T] + dot(sel9_ref[...], nine[:, cols2], 0, 0)


def combine_a(sel, sel9, y):
    whole = lambda j: (0, 0)
    return pl.pallas_call(
        combine_a_kernel,
        grid=(HALF // TN,),
        in_specs=[
            pl.BlockSpec((R8, 2 * T), whole),
            pl.BlockSpec((E, T), whole),
            pl.BlockSpec((R8, TN), lambda j: (0, j)),
            pl.BlockSpec((R8, FOLD), lambda j: (0, HALF // FOLD)),
        ],
        out_specs=pl.BlockSpec((2 * T, TN), lambda j: (0, j)),
        out_shape=jax.ShapeDtypeStruct((2 * T, HALF), F32),
        scratch_shapes=[
            pltpu.VMEM((FL, R8, LANE), F32),
            pltpu.VMEM((E, D), BF),
        ],
        compiler_params=ONE_DIM,
        cost_estimate=cost(2 * R8 * T * D, 2 * R8 * BACK_A + 4 * T * D),
        name="combine_a",
    )(sel, sel9, y, y)


CN = 256


def combine_b_kernel(
    ids_hbm, gates_hbm, mix_hbm, sel9_hbm, sel_t_hbm, part_hbm, y_hbm, out_hbm, gg_hbm,
    ids_ref, gates_ref, mix_ref, sel9_ref, sel_t_ref, part_ref, y_ref, out_ref, gg_ref,
    fold, in_sems, out_sems,
):
    pieces = HALF // CN

    def load(n, source, target):
        copy = pltpu.make_async_copy(source, target, in_sems.at[n])
        copy.start()
        return copy

    gate_cols = pl.ds(HALF, LANE)
    first = [
        load(0, sel_t_hbm, sel_t_ref),
        load(1, part_hbm, part_ref),
    ]
    parts = []
    for p in range(pieces):
        cols = pl.ds(p * CN, CN)
        parts.append(load(2 + p, y_hbm.at[:, cols], y_ref.at[:, cols]))
    rest = [
        load(2 + pieces, y_hbm.at[:, gate_cols], y_ref.at[:, gate_cols]),
        load(3 + pieces, mix_hbm, mix_ref),
        load(4 + pieces, sel9_hbm, sel9_ref),
        load(5 + pieces, ids_hbm, ids_ref),
        load(6 + pieces, gates_hbm, gates_ref),
    ]
    stores = []

    def send(source, target):
        store = pltpu.make_async_copy(source, target, out_sems.at[len(stores)])
        store.start()
        stores.append(store)

    for copy in first:
        copy.wait()
    for p in range(pieces):
        parts[p].wait()
        at = p * CN
        acc = part_ref[:, at : at + CN] + dot(sel_t_ref[...], y_ref[:, at : at + CN])
        out_ref[:, at : at + CN] = acc[0:T].astype(BF)
        out_ref[:, HALF + at : HALF + at + CN] = acc[T : 2 * T].astype(BF)
    send(out_ref, out_hbm)
    for copy in rest:
        copy.wait()
    fold[...] = y_ref[:, HALF:BACK_B].astype(F32)
    own = jnp.broadcast_to(fold[:, 0:1], (R8, T))
    picked = jnp.where(mix_ref[...].astype(F32) > 0.0, own, 0.0).reshape(E, SUB, T)
    ninth = jnp.broadcast_to(fold[pl.ds(0, E, stride=SUB), :][:, 1:2], (E, T))
    table = jnp.sum(picked, axis=1)
    table = table + jnp.where(sel9_ref[...].astype(F32) > 0.0, ninth, 0.0)
    expert = lax.broadcasted_iota(jnp.int32, (E, T), 0)
    totals = []
    for k in range(K):
        hit = ids_ref[k : k + 1, :] == expert
        totals.append(jnp.sum(jnp.where(hit, table, 0.0), axis=0, keepdims=True))
    total = jnp.concatenate(totals, axis=0) / gates_ref[...].astype(F32)
    gg_ref[...] = total.astype(BF)
    send(gg_ref, gg_hbm)
    for store in stores:
        store.wait()


def combine_b(ids_t, gates_t, mix, sel9, sel_t, part, y):
    return pl.pallas_call(
        combine_b_kernel,
        in_specs=[pl.BlockSpec(memory_space=pl.ANY)] * 7,
        out_specs=[pl.BlockSpec(memory_space=pl.ANY)] * 2,
        out_shape=[
            jax.ShapeDtypeStruct((T, D), BF),
            jax.ShapeDtypeStruct((K, T), BF),
        ],
        scratch_shapes=[
            pltpu.VMEM((K, T), jnp.int32),
            pltpu.VMEM((K, T), BF),
            pltpu.VMEM((R8, T), BF),
            pltpu.VMEM((E, T), BF),
            pltpu.VMEM((2 * T, R8), BF),
            pltpu.VMEM((2 * T, HALF), F32),
            pltpu.VMEM((R8, BACK_B), BF),
            pltpu.VMEM((T, D), BF),
            pltpu.VMEM((K, T), BF),
            pltpu.VMEM((R8, LANE), F32),
            pltpu.SemaphoreType.DMA((7 + HALF // CN,)),
            pltpu.SemaphoreType.DMA((2,)),
        ],
        cost_estimate=cost(2 * R8 * T * D, 2 * R8 * BACK_B + 4 * T * D),
        name="combine_b",
    )(ids_t, gates_t, mix, sel9, sel_t, part, y)


def exchange(x):
    width = x.shape[1]
    y = lax.all_to_all(
        x.reshape(E, SUB, width), AXES, split_axis=0, concat_axis=0, tiled=True
    )
    return y.reshape(R8, width)


def body(acts, out_grad, expert_ids, gate_vals, w_gate, w_up, w_down):
    ids_t = expert_ids.T
    gates_t = gate_vals.T
    wg, wu, wd = w_gate[0], w_up[0], w_down[0]
    send_a, sel_a, sel9, rank, gate = pack_a(ids_t, gates_t, acts, out_grad)
    got_a = exchange(send_a)
    send_b, sel_b_t, mix = pack_b(rank, gate, acts, out_grad)
    got_b = exchange(send_b)
    back_a, x_a, g_a, dpre_a, dup_a, hid_a, totals = expert_side(True, got_a, wg, wu, wd)
    wg_part = dot(x_a, dpre_a, 0, 0)
    wd_part = dot(hid_a, g_a, 0, 0)
    back_a, wg_part, wd_part = lax.optimization_barrier((back_a, wg_part, wd_part))
    home_a = exchange(back_a)
    back_b, x_b, g_b, dpre_b, dup_b, hid_b = expert_side(False, got_b, wg, wu, wd, totals)
    home_b = exchange(back_b)
    wg_grad = (wg_part + dot(x_b, dpre_b, 0, 0)).astype(BF)
    wu_grad = (dot(x_a, dup_a, 0, 0) + dot(x_b, dup_b, 0, 0)).astype(BF)
    wd_grad = (wd_part + dot(hid_b, g_b, 0, 0)).astype(BF)
    part = combine_a(sel_a, sel9, home_a)
    grad_acts, gate_grad_t = combine_b(ids_t, gates_t, mix, sel9, sel_b_t, part, home_b)
    return (
        grad_acts,
        gate_grad_t.T,
        wg_grad[None],
        wu_grad[None],
        wd_grad[None],
    )


def solution(mesh):
    rows = P(AXES, None)
    mats = P(AXES, None, None)
    return jax.shard_map(
        body,
        mesh=mesh,
        in_specs=(rows, rows, rows, rows, mats, mats, mats),
        out_specs=(rows, rows, mats, mats, mats),
        check_vma=False,
    )
```

```python
import functools

import jax
import jax.numpy as jnp
from jax import lax
from jax.experimental import pallas as pl
from jax.experimental.pallas import tpu as pltpu
from jax.sharding import PartitionSpec as P

AXES = ("grp", "loc")
BF = jnp.bfloat16
F32 = jnp.float32
E = 128
T = 128
K = 8
D = 2048
FF = 768
LANE = 128
SUB = 8
R8 = E * SUB
HALF = D // 2
HL = HALF // LANE
FOLD = D // SUB
FL = FOLD // LANE
GROUP = 4 * E
ROWS_A = GROUP + E
SEND_A = 2 * HALF + 2 * FOLD
SEND_B = 2 * HALF
BACK_A = HALF + FOLD
BACK_B = HALF + LANE
TN = 512
TF = 256
N1 = FF // TF
N2 = D // TN


def dot(a, b, ca=1, cb=0):
    return lax.dot_general(a, b, (((ca,), (cb,)), ((), ())), preferred_element_type=F32)


def cost(flops, bytes_accessed):
    return pl.CostEstimate(
        flops=int(flops), bytes_accessed=int(bytes_accessed), transcendentals=0
    )


ONE_DIM = pltpu.CompilerParams(dimension_semantics=("arbitrary",))
SINGLE = pl.Buffered(1)


def lanes(i):
    return slice(i * LANE, (i + 1) * LANE)


def halves(x, start, width):
    return jnp.concatenate(
        [x[:, start : start + width], x[:, HALF + start : HALF + start + width]], axis=0
    )


def pair_select(rank, weight, base):
    sub = lax.broadcasted_iota(jnp.int32, (E, SUB, T), 1)
    slot = (base + sub // 2).astype(F32)
    hit = jnp.where(rank[:, None, :] == slot, weight, 0.0)
    even = (sub % 2) == 0
    left = jnp.where(even, hit, 0.0).reshape(R8, T)
    right = jnp.where(even, 0.0, hit).reshape(R8, T)
    return jnp.concatenate([left, right], axis=1).astype(BF)


def pack_a_kernel(
    ids_hbm, gates_hbm, x_hbm, g_hbm, out_hbm, sel_hbm, sel9_hbm, rank_hbm, gate_hbm,
    ids_ref, gates_ref, x_ref, g_ref, sel_ref, sel9_ref, rank_ref, gate_ref,
    selg, fold, out, in_sems, out_sems,
):
    loads = [
        pltpu.make_async_copy(source, target, in_sems.at[n])
        for n, (source, target) in enumerate(
            (
                (ids_hbm, ids_ref),
                (gates_hbm, gates_ref),
                (x_hbm, x_ref),
                (g_hbm, g_ref),
            )
        )
    ]
    for load in loads:
        load.start()
    stores = []

    def send(source, target):
        store = pltpu.make_async_copy(source, target, out_sems.at[len(stores)])
        store.start()
        stores.append(store)

    def send_piece(piece):
        cols = pl.ds(piece * TN, TN)
        send(out.at[:, cols], out_hbm.at[:, cols])

    loads[0].wait()
    loads[1].wait()
    expert = lax.broadcasted_iota(jnp.int32, (E, T), 0)
    member = jnp.zeros((E, T), F32)
    gate = jnp.zeros((E, T), F32)
    for k in range(K):
        hit = ids_ref[k : k + 1, :] == expert
        member = jnp.where(hit, 1.0, member)
        gate = jnp.where(hit, gates_ref[k : k + 1, :].astype(F32), gate)
    earlier = (
        lax.broadcasted_iota(jnp.int32, (T, T), 0)
        < lax.broadcasted_iota(jnp.int32, (T, T), 1)
    ).astype(F32)
    rank = dot(member.astype(BF), earlier.astype(BF))
    rank = jnp.where(member > 0.0, rank, -1.0)
    rank_ref[...] = rank
    gate_ref[...] = gate
    sel9 = jnp.where(rank == float(SUB), 1.0, 0.0)
    sel9_ref[...] = sel9.astype(BF)
    sel9g = (sel9 * gate).astype(BF)
    sel_ref[...] = pair_select(rank, 1.0, 0)
    selg[...] = pair_select(rank, gate[:, None, :], 0)

    tiles = HALF // TN
    loads[2].wait()
    for c in range(tiles):
        out[:, c * TN : (c + 1) * TN] = dot(
            sel_ref[...], halves(x_ref, c * TN, TN)
        ).astype(BF)
        send_piece(c)
    loads[3].wait()
    for c in range(tiles):
        at = (tiles + 1 + c) * TN
        out[:, at : at + TN] = dot(selg[...], halves(g_ref, c * TN, TN)).astype(BF)
        send_piece(tiles + 1 + c)
    nine = dot(sel9_ref[...], x_ref[...])
    nine_g = dot(sel9g, g_ref[...])
    for i in range(SUB):
        rows = pl.ds(i, E, stride=SUB)
        for h in range(FL):
            at = i * FOLD + h * LANE
            fold[h, rows, :] = nine[:, at : at + LANE]
            fold[FL + h, rows, :] = nine_g[:, at : at + LANE]
    for h in range(2 * FL):
        at = HALF + h * LANE
        out[:, at : at + LANE] = fold[h].astype(BF)
    send_piece(tiles)
    send(sel_ref, sel_hbm)
    send(sel9_ref, sel9_hbm)
    send(rank_ref, rank_hbm)
    send(gate_ref, gate_hbm)
    for store in stores:
        store.wait()


def pack_a(ids_t, gates_t, acts, grad):
    return pl.pallas_call(
        pack_a_kernel,
        in_specs=[pl.BlockSpec(memory_space=pl.ANY)] * 4,
        out_specs=[pl.BlockSpec(memory_space=pl.ANY)] * 5,
        out_shape=[
            jax.ShapeDtypeStruct((R8, SEND_A), BF),
            jax.ShapeDtypeStruct((R8, 2 * T), BF),
            jax.ShapeDtypeStruct((E, T), BF),
            jax.ShapeDtypeStruct((E, T), F32),
            jax.ShapeDtypeStruct((E, T), F32),
        ],
        scratch_shapes=[
            pltpu.VMEM((K, T), jnp.int32),
            pltpu.VMEM((K, T), BF),
            pltpu.VMEM((T, D), BF),
            pltpu.VMEM((T, D), BF),
            pltpu.VMEM((R8, 2 * T), BF),
            pltpu.VMEM((E, T), BF),
            pltpu.VMEM((E, T), F32),
            pltpu.VMEM((E, T), F32),
            pltpu.VMEM((R8, 2 * T), BF),
            pltpu.VMEM((2 * FL, R8, LANE), F32),
            pltpu.VMEM((R8, SEND_A), BF),
            pltpu.SemaphoreType.DMA((4,)),
            pltpu.SemaphoreType.DMA((SEND_A // TN + 4,)),
        ],
        cost_estimate=cost(4 * R8 * T * D, 2 * R8 * SEND_A + 4 * T * D),
        name="pack_a",
    )(ids_t, gates_t, acts, grad)


def pack_b_kernel(rank_ref, gate_ref, x_ref, g_ref, out_ref, sel_t_ref, mix_ref, sel, selg):
    j = pl.program_id(0)
    tiles = HALF // TN

    @pl.when(j == 0)
    def _():
        rank = rank_ref[...]
        sel[...] = pair_select(rank, 1.0, 4)
        selg[...] = pair_select(rank, gate_ref[...][:, None, :], 4)
        sub = lax.broadcasted_iota(jnp.int32, (E, SUB, T), 1)
        slot = (sub // 2 + 4 * (sub % 2)).astype(F32)
        mix_ref[...] = jnp.where(rank[:, None, :] == slot, 1.0, 0.0).reshape(R8, T).astype(BF)

    @pl.when(j == 1)
    def _():
        sel_t_ref[...] = sel[...].T

    for c in range(tiles):

        @pl.when(j == c)
        def _():
            out_ref[...] = dot(sel[...], halves(x_ref, c * TN, TN)).astype(BF)

        @pl.when(j == tiles + c)
        def _():
            out_ref[...] = dot(selg[...], halves(g_ref, c * TN, TN)).astype(BF)


def pack_b(rank, gate, acts, grad):
    whole = lambda j: (0, 0)
    return pl.pallas_call(
        pack_b_kernel,
        grid=(SEND_B // TN,),
        in_specs=[
            pl.BlockSpec((E, T), whole),
            pl.BlockSpec((E, T), whole),
            pl.BlockSpec((T, D), whole),
            pl.BlockSpec((T, D), whole),
        ],
        out_specs=[
            pl.BlockSpec((R8, TN), lambda j: (0, j)),
            pl.BlockSpec((2 * T, R8), whole),
            pl.BlockSpec((R8, T), whole),
        ],
        out_shape=[
            jax.ShapeDtypeStruct((R8, SEND_B), BF),
            jax.ShapeDtypeStruct((2 * T, R8), BF),
            jax.ShapeDtypeStruct((R8, T), BF),
        ],
        scratch_shapes=[pltpu.VMEM((R8, 2 * T), BF), pltpu.VMEM((R8, 2 * T), BF)],
        compiler_params=ONE_DIM,
        cost_estimate=cost(4 * R8 * T * D, 2 * R8 * SEND_B + 4 * T * D),
        name="pack_b",
    )(rank, gate, acts, grad)


def expert_kernel(
    nine, y_ref, wg_ref, wu_ref, wd_ref, wg2_ref, wu2_ref, *rest
):
    if nine:
        out_ref, x_ref, g_ref, dpre_ref, dup_ref, hid_ref, tot_ref, fold, gsum = rest
    else:
        tot_ref, out_ref, x_ref, g_ref, dpre_ref, dup_ref, hid_ref, fold, gsum = rest
    i = pl.program_id(0)
    rows_all = GROUP + (E if nine else 0)
    step = rows_all // 2
    after = HALF + (2 * FOLD if nine else 0)

    def unfold(base, base9, rows_ref):
        for c in range(HL):
            at = base + c * LANE
            fold[c] = y_ref[:, at : at + LANE].astype(F32)
            for h in range(2):
                to = h * HALF + c * LANE
                rows_ref[0:GROUP, to : to + LANE] = fold[
                    c, pl.ds(h, GROUP, stride=2), :
                ].astype(BF)
        if nine:
            for h in range(FL):
                at = base9 + h * LANE
                fold[h] = y_ref[:, at : at + LANE].astype(F32)
            for s in range(SUB):
                for h in range(FL):
                    to = s * FOLD + h * LANE
                    rows_ref[GROUP:rows_all, to : to + LANE] = fold[
                        h, pl.ds(s, E, stride=SUB), :
                    ].astype(BF)

    @pl.when(i == 0)
    def _():
        unfold(0, HALF, x_ref)
        unfold(after, HALF + FOLD, g_ref)
        gsum[...] = jnp.zeros_like(gsum)

    @pl.when(i < N1)
    def _():
        cols = pl.ds(pl.multiple_of(jnp.minimum(i, N1 - 1) * TF, TF), TF)
        for m in range(2):
            rows = pl.ds(m * step, step)
            x = x_ref[rows, :]
            pre = dot(x, wg_ref[...])
            up = dot(x, wu_ref[...])
            dh = dot(g_ref[rows, :], wd_ref[...], 1, 1)
            s = jax.nn.sigmoid(pre)
            act = pre * s
            hid = act * up
            part = hid * dh
            gsum[rows, :] += part[:, 0:LANE] + part[:, LANE:TF]
            hid_ref[rows, cols] = hid.astype(BF)
            dup_ref[rows, cols] = (dh * act).astype(BF)
            dpre_ref[rows, cols] = (dh * up * s * (1.0 + pre * (1.0 - s))).astype(BF)

    @pl.when((i >= N1) & (i < N1 + N2))
    def _():
        j = i - N1
        half = j // 2
        for m in range(2):
            rows = pl.ds(m * step, step)
            dx = dot(dpre_ref[rows, :], wg2_ref[...], 1, 1)
            dx = dx + dot(dup_ref[rows, :], wu2_ref[...], 1, 1)
            keep = min(step, GROUP - m * step)
            for q in range(TN // LANE):
                fold[
                    (j % 2) * (TN // LANE) + q,
                    pl.ds(2 * m * step + half, keep, stride=2),
                    :,
                ] = dx[0:keep, lanes(q)]
            if keep < step:
                for q in range(TN // LANE):
                    fold[HL + q % FL, pl.ds(j * (TN // FOLD) + q // FL, E, stride=SUB), :] = dx[
                        keep:step, lanes(q)
                    ]

    @pl.when(i == N1 + N2)
    def _():
        for c in range(HL + (FL if nine else 0)):
            out_ref[:, lanes(c)] = fold[c].astype(BF)
        total = jnp.sum(gsum[...], axis=1, keepdims=True)
        total = jnp.broadcast_to(total, (rows_all, LANE))
        if nine:
            tot_ref[...] = total
        else:
            fold[0, pl.ds(0, GROUP, stride=2), :] = tot_ref[0:GROUP, :]
            fold[0, pl.ds(1, GROUP, stride=2), :] = total
            for s in range(SUB):
                fold[1, pl.ds(s, E, stride=SUB), :] = tot_ref[GROUP:ROWS_A, :]
            lane = lax.broadcasted_iota(jnp.int32, (R8, LANE), 1)
            out_ref[:, lanes(HL)] = jnp.where(lane == 1, fold[1], fold[0]).astype(BF)


def expert_side(nine, y, wg, wu, wd, *totals):
    rows_all = GROUP + (E if nine else 0)
    send, back = (SEND_A, BACK_A) if nine else (SEND_B, BACK_B)
    first = lambda i: (0, jnp.minimum(i, N1 - 1))
    second = lambda i: (jnp.clip(i - N1, 0, N2 - 1), 0)
    whole = lambda i: (0, 0)
    return pl.pallas_call(
        functools.partial(expert_kernel, nine),
        grid=(N1 + N2 + 1,),
        in_specs=[
            pl.BlockSpec((R8, send), whole, pipeline_mode=SINGLE),
            pl.BlockSpec((D, TF), first),
            pl.BlockSpec((D, TF), first),
            pl.BlockSpec((TF, D), lambda i: (jnp.minimum(i, N1 - 1), 0)),
            pl.BlockSpec((TN, FF), second),
            pl.BlockSpec((TN, FF), second),
        ]
        + [pl.BlockSpec((ROWS_A, LANE), whole) for _ in totals],
        out_specs=[
            pl.BlockSpec((R8, back), whole, pipeline_mode=SINGLE),
            pl.BlockSpec((rows_all, D), whole, pipeline_mode=SINGLE),
            pl.BlockSpec((rows_all, D), whole, pipeline_mode=SINGLE),
            pl.BlockSpec((rows_all, FF), whole, pipeline_mode=SINGLE),
            pl.BlockSpec((rows_all, FF), whole, pipeline_mode=SINGLE),
            pl.BlockSpec((rows_all, FF), whole, pipeline_mode=SINGLE),
        ]
        + [pl.BlockSpec((ROWS_A, LANE), whole)] * nine,
        out_shape=[
            jax.ShapeDtypeStruct((R8, back), BF),
            jax.ShapeDtypeStruct((rows_all, D), BF),
            jax.ShapeDtypeStruct((rows_all, D), BF),
            jax.ShapeDtypeStruct((rows_all, FF), BF),
            jax.ShapeDtypeStruct((rows_all, FF), BF),
            jax.ShapeDtypeStruct((rows_all, FF), BF),
        ]
        + [jax.ShapeDtypeStruct((ROWS_A, LANE), F32)] * nine,
        scratch_shapes=[
            pltpu.VMEM((HL + FL, R8, LANE), F32),
            pltpu.VMEM((rows_all, LANE), F32),
        ],
        compiler_params=ONE_DIM,
        cost_estimate=cost(10 * rows_all * D * FF, 40e6),
        name="expert_a" if nine else "expert_b",
    )(y, wg, wu, wd, wg, wu, *totals)


def combine_a_kernel(sel_ref, sel9_ref, y_ref, y9_ref, out_ref, fold, nine):
    j = pl.program_id(0)

    @pl.when(j == 0)
    def _():
        for h in range(FL):
            fold[h] = y9_ref[:, lanes(h)].astype(F32)
        for s in range(SUB):
            for h in range(FL):
                at = s * FOLD + h * LANE
                nine[:, at : at + LANE] = fold[h, pl.ds(s, E, stride=SUB), :].astype(BF)

    acc = dot(sel_ref[...], y_ref[...], 0, 0)
    cols = pl.ds(pl.multiple_of(j * TN, TN), TN)
    cols2 = pl.ds(pl.multiple_of(HALF + j * TN, TN), TN)
    out_ref[0:T, :] = acc[0:T] + dot(sel9_ref[...], nine[:, cols], 0, 0)
    out_ref[T : 2 * T, :] = acc[T : 2 * T] + dot(sel9_ref[...], nine[:, cols2], 0, 0)


def combine_a(sel, sel9, y):
    whole = lambda j: (0, 0)
    return pl.pallas_call(
        combine_a_kernel,
        grid=(HALF // TN,),
        in_specs=[
            pl.BlockSpec((R8, 2 * T), whole),
            pl.BlockSpec((E, T), whole),
            pl.BlockSpec((R8, TN), lambda j: (0, j)),
            pl.BlockSpec((R8, FOLD), lambda j: (0, HALF // FOLD)),
        ],
        out_specs=pl.BlockSpec((2 * T, TN), lambda j: (0, j)),
        out_shape=jax.ShapeDtypeStruct((2 * T, HALF), F32),
        scratch_shapes=[
            pltpu.VMEM((FL, R8, LANE), F32),
            pltpu.VMEM((E, D), BF),
        ],
        compiler_params=ONE_DIM,
        cost_estimate=cost(2 * R8 * T * D, 2 * R8 * BACK_A + 4 * T * D),
        name="combine_a",
    )(sel, sel9, y, y)


CN = 512


def combine_b_kernel(
    ids_hbm, gates_hbm, mix_hbm, sel9_hbm, sel_t_hbm, part_hbm, y_hbm, out_hbm, gg_hbm,
    ids_ref, gates_ref, mix_ref, sel9_ref, sel_t_ref, part_ref, y_ref, out_ref, gg_ref,
    fold, in_sems, out_sems,
):
    pieces = HALF // CN
    count = iter(range(7 + 2 * pieces))

    def load(source, target):
        copy = pltpu.make_async_copy(source, target, in_sems.at[next(count)])
        copy.start()
        return copy

    gate_cols = pl.ds(HALF, LANE)
    small = [
        load(ids_hbm, ids_ref),
        load(gates_hbm, gates_ref),
        load(sel9_hbm, sel9_ref),
        load(y_hbm.at[:, gate_cols], y_ref.at[:, gate_cols]),
        load(mix_hbm, mix_ref),
    ]
    first = load(sel_t_hbm, sel_t_ref)
    parts = []
    for p in range(pieces):
        cols = pl.ds(p * CN, CN)
        parts.append(
            [
                load(y_hbm.at[:, cols], y_ref.at[:, cols]),
                load(part_hbm.at[:, cols], part_ref.at[:, cols]),
            ]
        )
    stores = []

    def send(source, target):
        store = pltpu.make_async_copy(source, target, out_sems.at[len(stores)])
        store.start()
        stores.append(store)

    for copy in small:
        copy.wait()
    fold[...] = y_ref[:, HALF:BACK_B].astype(F32)
    own = jnp.broadcast_to(fold[:, 0:1], (R8, T))
    picked = jnp.where(mix_ref[...].astype(F32) > 0.0, own, 0.0).reshape(E, SUB, T)
    ninth = jnp.broadcast_to(fold[pl.ds(0, E, stride=SUB), :][:, 1:2], (E, T))
    table = jnp.sum(picked, axis=1)
    table = table + jnp.where(sel9_ref[...].astype(F32) > 0.0, ninth, 0.0)
    expert = lax.broadcasted_iota(jnp.int32, (E, T), 0)
    totals = []
    for k in range(K):
        hit = ids_ref[k : k + 1, :] == expert
        totals.append(jnp.sum(jnp.where(hit, table, 0.0), axis=0, keepdims=True))
    total = jnp.concatenate(totals, axis=0) / gates_ref[...].astype(F32)
    gg_ref[...] = total.astype(BF)
    send(gg_ref, gg_hbm)
    first.wait()
    for p in range(pieces):
        for copy in parts[p]:
            copy.wait()
        at = p * CN
        acc = part_ref[:, at : at + CN] + dot(sel_t_ref[...], y_ref[:, at : at + CN])
        out_ref[:, at : at + CN] = acc[0:T].astype(BF)
        out_ref[:, HALF + at : HALF + at + CN] = acc[T : 2 * T].astype(BF)
        for start in (at, HALF + at):
            cols = pl.ds(start, CN)
            send(out_ref.at[:, cols], out_hbm.at[:, cols])
    for store in stores:
        store.wait()


def combine_b(ids_t, gates_t, mix, sel9, sel_t, part, y):
    return pl.pallas_call(
        combine_b_kernel,
        in_specs=[pl.BlockSpec(memory_space=pl.ANY)] * 7,
        out_specs=[pl.BlockSpec(memory_space=pl.ANY)] * 2,
        out_shape=[
            jax.ShapeDtypeStruct((T, D), BF),
            jax.ShapeDtypeStruct((K, T), BF),
        ],
        scratch_shapes=[
            pltpu.VMEM((K, T), jnp.int32),
            pltpu.VMEM((K, T), BF),
            pltpu.VMEM((R8, T), BF),
            pltpu.VMEM((E, T), BF),
            pltpu.VMEM((2 * T, R8), BF),
            pltpu.VMEM((2 * T, HALF), F32),
            pltpu.VMEM((R8, BACK_B), BF),
            pltpu.VMEM((T, D), BF),
            pltpu.VMEM((K, T), BF),
            pltpu.VMEM((R8, LANE), F32),
            pltpu.SemaphoreType.DMA((7 + 2 * HALF // CN,)),
            pltpu.SemaphoreType.DMA((1 + 2 * HALF // CN,)),
        ],
        cost_estimate=cost(2 * R8 * T * D, 2 * R8 * BACK_B + 4 * T * D),
        name="combine_b",
    )(ids_t, gates_t, mix, sel9, sel_t, part, y)


def exchange(x):
    width = x.shape[1]
    y = lax.all_to_all(
        x.reshape(E, SUB, width), AXES, split_axis=0, concat_axis=0, tiled=True
    )
    return y.reshape(R8, width)


def body(acts, out_grad, expert_ids, gate_vals, w_gate, w_up, w_down):
    ids_t = expert_ids.T
    gates_t = gate_vals.T
    wg, wu, wd = w_gate[0], w_up[0], w_down[0]
    send_a, sel_a, sel9, rank, gate = pack_a(ids_t, gates_t, acts, out_grad)
    got_a = exchange(send_a)
    send_b, sel_b_t, mix = pack_b(rank, gate, acts, out_grad)
    got_b = exchange(send_b)
    back_a, x_a, g_a, dpre_a, dup_a, hid_a, totals = expert_side(True, got_a, wg, wu, wd)
    wg_part = dot(x_a, dpre_a, 0, 0)
    wd_part = dot(hid_a, g_a, 0, 0)
    back_a, wg_part, wd_part = lax.optimization_barrier((back_a, wg_part, wd_part))
    home_a = exchange(back_a)
    back_b, x_b, g_b, dpre_b, dup_b, hid_b = expert_side(False, got_b, wg, wu, wd, totals)
    home_b = exchange(back_b)
    wg_grad = (wg_part + dot(x_b, dpre_b, 0, 0)).astype(BF)
    wu_grad = (dot(x_a, dup_a, 0, 0) + dot(x_b, dup_b, 0, 0)).astype(BF)
    wd_grad = (wd_part + dot(hid_b, g_b, 0, 0)).astype(BF)
    part = combine_a(sel_a, sel9, home_a)
    grad_acts, gate_grad_t = combine_b(ids_t, gates_t, mix, sel9, sel_b_t, part, home_b)
    return (
        grad_acts,
        gate_grad_t.T,
        wg_grad[None],
        wu_grad[None],
        wd_grad[None],
    )


def solution(mesh):
    rows = P(AXES, None)
    mats = P(AXES, None, None)
    return jax.shard_map(
        body,
        mesh=mesh,
        in_specs=(rows, rows, rows, rows, mats, mats, mats),
        out_specs=(rows, rows, mats, mats, mats),
        check_vma=False,
    )
```

```python
import functools

import jax
import jax.numpy as jnp
from jax import lax
from jax.experimental import pallas as pl
from jax.experimental.pallas import tpu as pltpu
from jax.sharding import PartitionSpec as P

AXES = ("grp", "loc")
BF = jnp.bfloat16
F32 = jnp.float32
E = 128
T = 128
K = 8
D = 2048
FF = 768
LANE = 128
SUB = 8
R8 = E * SUB
HALF = D // 2
HL = HALF // LANE
FOLD = D // SUB
FL = FOLD // LANE
GROUP = 4 * E
ROWS_A = GROUP + E
ROWS_WIDE = 2 * HALF + 2 * FOLD
SEND_A = ROWS_WIDE + LANE
SEND_B = 2 * HALF
BACK_A = HALF + FOLD
BACK_B = HALF + LANE
TN = 512
TF = 256
N1 = FF // TF
N2 = D // TN


def dot(a, b, ca=1, cb=0):
    return lax.dot_general(a, b, (((ca,), (cb,)), ((), ())), preferred_element_type=F32)


def cost(flops, bytes_accessed):
    return pl.CostEstimate(
        flops=int(flops), bytes_accessed=int(bytes_accessed), transcendentals=0
    )


ONE_DIM = pltpu.CompilerParams(dimension_semantics=("arbitrary",))
SINGLE = pl.Buffered(1)


def lanes(i):
    return slice(i * LANE, (i + 1) * LANE)


def halves(x, start, width):
    return jnp.concatenate(
        [x[:, start : start + width], x[:, HALF + start : HALF + start + width]], axis=0
    )


def pair_select(rank, weight, base):
    sub = lax.broadcasted_iota(jnp.int32, (E, SUB, T), 1)
    slot = (base + sub // 2).astype(F32)
    hit = jnp.where(rank[:, None, :] == slot, weight, 0.0)
    even = (sub % 2) == 0
    left = jnp.where(even, hit, 0.0).reshape(R8, T)
    right = jnp.where(even, 0.0, hit).reshape(R8, T)
    return jnp.concatenate([left, right], axis=1).astype(BF)


def mix_rows(rank):
    sub = lax.broadcasted_iota(jnp.int32, (E, SUB, T), 1)
    slot = (sub // 2 + 4 * (sub % 2)).astype(F32)
    return rank[:, None, :] == slot


def pack_a_kernel(
    ids_hbm, gates_hbm, x_hbm, g_hbm, out_hbm, sel_hbm, sel9_hbm, rank_hbm,
    ids_ref, gates_ref, x_ref, g_ref, sel_ref, sel9_ref, rank_ref,
    fold, out, in_sems, out_sems,
):
    loads = [
        pltpu.make_async_copy(source, target, in_sems.at[n])
        for n, (source, target) in enumerate(
            (
                (ids_hbm, ids_ref),
                (gates_hbm, gates_ref),
                (x_hbm, x_ref),
                (g_hbm, g_ref),
            )
        )
    ]
    for load in loads:
        load.start()
    stores = []

    def send(source, target):
        store = pltpu.make_async_copy(source, target, out_sems.at[len(stores)])
        store.start()
        stores.append(store)

    def send_piece(piece):
        cols = pl.ds(piece * TN, TN)
        send(out.at[:, cols], out_hbm.at[:, cols])

    loads[0].wait()
    loads[1].wait()
    expert = lax.broadcasted_iota(jnp.int32, (E, T), 0)
    member = jnp.zeros((E, T), F32)
    gate = jnp.zeros((E, T), F32)
    for k in range(K):
        hit = ids_ref[k : k + 1, :] == expert
        member = jnp.where(hit, 1.0, member)
        gate = jnp.where(hit, gates_ref[k : k + 1, :].astype(F32), gate)
    earlier = (
        lax.broadcasted_iota(jnp.int32, (T, T), 0)
        < lax.broadcasted_iota(jnp.int32, (T, T), 1)
    ).astype(F32)
    rank = dot(member.astype(BF), earlier.astype(BF))
    rank = jnp.where(member > 0.0, rank, -1.0)
    rank_ref[...] = rank
    sel9 = jnp.where(rank == float(SUB), 1.0, 0.0)
    sel9_ref[...] = sel9.astype(BF)
    sel_ref[...] = pair_select(rank, 1.0, 0)

    tiles = HALF // TN
    loads[2].wait()
    for c in range(tiles):
        out[:, c * TN : (c + 1) * TN] = dot(
            sel_ref[...], halves(x_ref, c * TN, TN)
        ).astype(BF)
        send_piece(c)
    loads[3].wait()
    for c in range(tiles):
        at = (tiles + 1 + c) * TN
        out[:, at : at + TN] = dot(sel_ref[...], halves(g_ref, c * TN, TN)).astype(BF)
        send_piece(tiles + 1 + c)
    nine = dot(sel9_ref[...], x_ref[...])
    nine_g = dot(sel9_ref[...], g_ref[...])
    for i in range(SUB):
        rows = pl.ds(i, E, stride=SUB)
        for h in range(FL):
            at = i * FOLD + h * LANE
            fold[h, rows, :] = nine[:, at : at + LANE]
            fold[FL + h, rows, :] = nine_g[:, at : at + LANE]
    for h in range(2 * FL):
        at = HALF + h * LANE
        out[:, at : at + LANE] = fold[h].astype(BF)
    send_piece(tiles)
    ones = jnp.ones((T, LANE), BF)
    mixed = jnp.where(mix_rows(rank), gate[:, None, :], 0.0).reshape(R8, T)
    own = dot(mixed.astype(BF), ones)
    ninth = dot((sel9 * gate).astype(BF), ones)
    ninth = jnp.broadcast_to(ninth[:, None, :], (E, SUB, LANE)).reshape(R8, LANE)
    lane = lax.broadcasted_iota(jnp.int32, (R8, LANE), 1)
    out[:, ROWS_WIDE:SEND_A] = jnp.where(lane == 1, ninth, own).astype(BF)
    last = pl.ds(ROWS_WIDE, LANE)
    send(out.at[:, last], out_hbm.at[:, last])
    send(sel_ref, sel_hbm)
    send(sel9_ref, sel9_hbm)
    send(rank_ref, rank_hbm)
    for store in stores:
        store.wait()


def pack_a(ids_t, gates_t, acts, grad):
    return pl.pallas_call(
        pack_a_kernel,
        in_specs=[pl.BlockSpec(memory_space=pl.ANY)] * 4,
        out_specs=[pl.BlockSpec(memory_space=pl.ANY)] * 4,
        out_shape=[
            jax.ShapeDtypeStruct((R8, SEND_A), BF),
            jax.ShapeDtypeStruct((R8, 2 * T), BF),
            jax.ShapeDtypeStruct((E, T), BF),
            jax.ShapeDtypeStruct((E, T), F32),
        ],
        scratch_shapes=[
            pltpu.VMEM((K, T), jnp.int32),
            pltpu.VMEM((K, T), BF),
            pltpu.VMEM((T, D), BF),
            pltpu.VMEM((T, D), BF),
            pltpu.VMEM((R8, 2 * T), BF),
            pltpu.VMEM((E, T), BF),
            pltpu.VMEM((E, T), F32),
            pltpu.VMEM((2 * FL, R8, LANE), F32),
            pltpu.VMEM((R8, SEND_A), BF),
            pltpu.SemaphoreType.DMA((4,)),
            pltpu.SemaphoreType.DMA((ROWS_WIDE // TN + 5,)),
        ],
        cost_estimate=cost(4 * R8 * T * D, 2 * R8 * SEND_A + 4 * T * D),
        name="pack_a",
    )(ids_t, gates_t, acts, grad)


def pack_b_kernel(rank_ref, x_ref, g_ref, out_ref, sel_t_ref, mix_ref, sel):
    j = pl.program_id(0)
    tiles = HALF // TN

    @pl.when(j == 0)
    def _():
        rank = rank_ref[...]
        sel[...] = pair_select(rank, 1.0, 4)
        mix_ref[...] = jnp.where(mix_rows(rank), 1.0, 0.0).reshape(R8, T).astype(BF)

    @pl.when(j == 1)
    def _():
        sel_t_ref[...] = sel[...].T

    for c in range(tiles):

        @pl.when(j == c)
        def _():
            out_ref[...] = dot(sel[...], halves(x_ref, c * TN, TN)).astype(BF)

        @pl.when(j == tiles + c)
        def _():
            out_ref[...] = dot(sel[...], halves(g_ref, c * TN, TN)).astype(BF)


def pack_b(rank, acts, grad):
    whole = lambda j: (0, 0)
    return pl.pallas_call(
        pack_b_kernel,
        grid=(SEND_B // TN,),
        in_specs=[
            pl.BlockSpec((E, T), whole),
            pl.BlockSpec((T, D), whole),
            pl.BlockSpec((T, D), whole),
        ],
        out_specs=[
            pl.BlockSpec((R8, TN), lambda j: (0, j)),
            pl.BlockSpec((2 * T, R8), whole),
            pl.BlockSpec((R8, T), whole),
        ],
        out_shape=[
            jax.ShapeDtypeStruct((R8, SEND_B), BF),
            jax.ShapeDtypeStruct((2 * T, R8), BF),
            jax.ShapeDtypeStruct((R8, T), BF),
        ],
        scratch_shapes=[pltpu.VMEM((R8, 2 * T), BF)],
        compiler_params=ONE_DIM,
        cost_estimate=cost(4 * R8 * T * D, 2 * R8 * SEND_B + 4 * T * D),
        name="pack_b",
    )(rank, acts, grad)


def expert_kernel(
    nine, y_ref, gates_ref, wg_ref, wu_ref, wd_ref, wg2_ref, wu2_ref, *rest
):
    if nine:
        out_ref, x_ref, g_ref, dpre_ref, dup_ref, hid_ref, tot_ref, fold, gsum, gcol = rest
    else:
        tot_ref, out_ref, x_ref, g_ref, dpre_ref, dup_ref, hid_ref, fold, gsum, gcol = rest
    i = pl.program_id(0)
    rows_all = GROUP + (E if nine else 0)
    step = rows_all // 2
    after = HALF + (2 * FOLD if nine else 0)

    def unfold(base, base9, rows_ref):
        for c in range(HL):
            at = base + c * LANE
            fold[c] = y_ref[:, at : at + LANE].astype(F32)
            for h in range(2):
                to = h * HALF + c * LANE
                rows_ref[0:GROUP, to : to + LANE] = fold[
                    c, pl.ds(h, GROUP, stride=2), :
                ].astype(BF)
        if nine:
            for h in range(FL):
                at = base9 + h * LANE
                fold[h] = y_ref[:, at : at + LANE].astype(F32)
            for s in range(SUB):
                for h in range(FL):
                    to = s * FOLD + h * LANE
                    rows_ref[GROUP:rows_all, to : to + LANE] = fold[
                        h, pl.ds(s, E, stride=SUB), :
                    ].astype(BF)

    @pl.when(i == 0)
    def _():
        unfold(0, HALF, x_ref)
        unfold(after, HALF + FOLD, g_ref)
        gsum[...] = jnp.zeros_like(gsum)
        fold[0] = gates_ref[...].astype(F32)
        own = fold[0, pl.ds(0 if nine else 1, GROUP, stride=2), :]
        gcol[0:GROUP, :] = jnp.broadcast_to(own[:, 0:1], (GROUP, LANE))
        if nine:
            ninth = fold[0, pl.ds(0, E, stride=SUB), :]
            gcol[GROUP:rows_all, :] = jnp.broadcast_to(ninth[:, 1:2], (E, LANE))

    @pl.when(i < N1)
    def _():
        cols = pl.ds(pl.multiple_of(jnp.minimum(i, N1 - 1) * TF, TF), TF)
        for m in range(2):
            rows = pl.ds(m * step, step)
            x = x_ref[rows, :]
            pre = dot(x, wg_ref[...])
            up = dot(x, wu_ref[...])
            dh = dot(g_ref[rows, :], wd_ref[...], 1, 1)
            s = jax.nn.sigmoid(pre)
            act = pre * s
            hid = act * up
            part = hid * dh
            gsum[rows, :] += part[:, 0:LANE] + part[:, LANE:TF]
            gate = jnp.concatenate([gcol[rows, :]] * (TF // LANE), axis=1)
            hid_ref[rows, cols] = (gate * hid).astype(BF)
            dh = gate * dh
            dup_ref[rows, cols] = (dh * act).astype(BF)
            dpre_ref[rows, cols] = (dh * up * s * (1.0 + pre * (1.0 - s))).astype(BF)

    @pl.when((i >= N1) & (i < N1 + N2))
    def _():
        j = i - N1
        half = j // 2
        for m in range(2):
            rows = pl.ds(m * step, step)
            dx = dot(dpre_ref[rows, :], wg2_ref[...], 1, 1)
            dx = dx + dot(dup_ref[rows, :], wu2_ref[...], 1, 1)
            keep = min(step, GROUP - m * step)
            for q in range(TN // LANE):
                fold[
                    (j % 2) * (TN // LANE) + q,
                    pl.ds(2 * m * step + half, keep, stride=2),
                    :,
                ] = dx[0:keep, lanes(q)]
            if keep < step:
                for q in range(TN // LANE):
                    fold[HL + q % FL, pl.ds(j * (TN // FOLD) + q // FL, E, stride=SUB), :] = dx[
                        keep:step, lanes(q)
                    ]

    @pl.when(i == N1 + N2)
    def _():
        for c in range(HL + (FL if nine else 0)):
            out_ref[:, lanes(c)] = fold[c].astype(BF)
        total = jnp.sum(gsum[...], axis=1, keepdims=True)
        total = jnp.broadcast_to(total, (rows_all, LANE))
        if nine:
            tot_ref[...] = total
        else:
            fold[0, pl.ds(0, GROUP, stride=2), :] = tot_ref[0:GROUP, :]
            fold[0, pl.ds(1, GROUP, stride=2), :] = total
            for s in range(SUB):
                fold[1, pl.ds(s, E, stride=SUB), :] = tot_ref[GROUP:ROWS_A, :]
            lane = lax.broadcasted_iota(jnp.int32, (R8, LANE), 1)
            out_ref[:, lanes(HL)] = jnp.where(lane == 1, fold[1], fold[0]).astype(BF)


def expert_side(nine, y, gates, wg, wu, wd, *totals):
    rows_all = GROUP + (E if nine else 0)
    send, back = (SEND_A, BACK_A) if nine else (SEND_B, BACK_B)
    first = lambda i: (0, jnp.minimum(i, N1 - 1))
    second = lambda i: (jnp.clip(i - N1, 0, N2 - 1), 0)
    whole = lambda i: (0, 0)
    return pl.pallas_call(
        functools.partial(expert_kernel, nine),
        grid=(N1 + N2 + 1,),
        in_specs=[
            pl.BlockSpec((R8, ROWS_WIDE if nine else send), whole, pipeline_mode=SINGLE),
            pl.BlockSpec((R8, LANE), lambda i: (0, ROWS_WIDE // LANE)),
            pl.BlockSpec((D, TF), first),
            pl.BlockSpec((D, TF), first),
            pl.BlockSpec((TF, D), lambda i: (jnp.minimum(i, N1 - 1), 0)),
            pl.BlockSpec((TN, FF), second),
            pl.BlockSpec((TN, FF), second),
        ]
        + [pl.BlockSpec((ROWS_A, LANE), whole) for _ in totals],
        out_specs=[
            pl.BlockSpec((R8, back), whole, pipeline_mode=SINGLE),
            pl.BlockSpec((rows_all, D), whole, pipeline_mode=SINGLE),
            pl.BlockSpec((rows_all, D), whole, pipeline_mode=SINGLE),
            pl.BlockSpec((rows_all, FF), whole, pipeline_mode=SINGLE),
            pl.BlockSpec((rows_all, FF), whole, pipeline_mode=SINGLE),
            pl.BlockSpec((rows_all, FF), whole, pipeline_mode=SINGLE),
        ]
        + [pl.BlockSpec((ROWS_A, LANE), whole)] * nine,
        out_shape=[
            jax.ShapeDtypeStruct((R8, back), BF),
            jax.ShapeDtypeStruct((rows_all, D), BF),
            jax.ShapeDtypeStruct((rows_all, D), BF),
            jax.ShapeDtypeStruct((rows_all, FF), BF),
            jax.ShapeDtypeStruct((rows_all, FF), BF),
            jax.ShapeDtypeStruct((rows_all, FF), BF),
        ]
        + [jax.ShapeDtypeStruct((ROWS_A, LANE), F32)] * nine,
        scratch_shapes=[
            pltpu.VMEM((HL + FL, R8, LANE), F32),
            pltpu.VMEM((rows_all, LANE), F32),
            pltpu.VMEM((rows_all, LANE), F32),
        ],
        compiler_params=ONE_DIM,
        cost_estimate=cost(10 * rows_all * D * FF, 40e6),
        name="expert_a" if nine else "expert_b",
    )(y, gates, wg, wu, wd, wg, wu, *totals)


def combine_a_kernel(sel_ref, sel9_ref, y_ref, y9_ref, out_ref, fold, nine):
    j = pl.program_id(0)

    @pl.when(j == 0)
    def _():
        for h in range(FL):
            fold[h] = y9_ref[:, lanes(h)].astype(F32)
        for s in range(SUB):
            for h in range(FL):
                at = s * FOLD + h * LANE
                nine[:, at : at + LANE] = fold[h, pl.ds(s, E, stride=SUB), :].astype(BF)

    acc = dot(sel_ref[...], y_ref[...], 0, 0)
    cols = pl.ds(pl.multiple_of(j * TN, TN), TN)
    cols2 = pl.ds(pl.multiple_of(HALF + j * TN, TN), TN)
    out_ref[0:T, :] = acc[0:T] + dot(sel9_ref[...], nine[:, cols], 0, 0)
    out_ref[T : 2 * T, :] = acc[T : 2 * T] + dot(sel9_ref[...], nine[:, cols2], 0, 0)


def combine_a(sel, sel9, y):
    whole = lambda j: (0, 0)
    return pl.pallas_call(
        combine_a_kernel,
        grid=(HALF // TN,),
        in_specs=[
            pl.BlockSpec((R8, 2 * T), whole),
            pl.BlockSpec((E, T), whole),
            pl.BlockSpec((R8, TN), lambda j: (0, j)),
            pl.BlockSpec((R8, FOLD), lambda j: (0, HALF // FOLD)),
        ],
        out_specs=pl.BlockSpec((2 * T, TN), lambda j: (0, j)),
        out_shape=jax.ShapeDtypeStruct((2 * T, HALF), F32),
        scratch_shapes=[
            pltpu.VMEM((FL, R8, LANE), F32),
            pltpu.VMEM((E, D), BF),
        ],
        compiler_params=ONE_DIM,
        cost_estimate=cost(2 * R8 * T * D, 2 * R8 * BACK_A + 4 * T * D),
        name="combine_a",
    )(sel, sel9, y, y)


CN = 512


def combine_b_kernel(
    ids_hbm, mix_hbm, sel9_hbm, sel_t_hbm, part_hbm, y_hbm, out_hbm, gg_hbm,
    ids_ref, mix_ref, sel9_ref, sel_t_ref, part_ref, y_ref, out_ref, gg_ref,
    fold, in_sems, out_sems,
):
    pieces = HALF // CN
    count = iter(range(7 + 2 * pieces))

    def load(source, target):
        copy = pltpu.make_async_copy(source, target, in_sems.at[next(count)])
        copy.start()
        return copy

    gate_cols = pl.ds(HALF, LANE)
    small = [
        load(ids_hbm, ids_ref),
        load(sel9_hbm, sel9_ref),
        load(y_hbm.at[:, gate_cols], y_ref.at[:, gate_cols]),
        load(mix_hbm, mix_ref),
    ]
    first = load(sel_t_hbm, sel_t_ref)
    parts = []
    for p in range(pieces):
        cols = pl.ds(p * CN, CN)
        parts.append(
            [
                load(y_hbm.at[:, cols], y_ref.at[:, cols]),
                load(part_hbm.at[:, cols], part_ref.at[:, cols]),
            ]
        )
    stores = []

    def send(source, target):
        store = pltpu.make_async_copy(source, target, out_sems.at[len(stores)])
        store.start()
        stores.append(store)

    for copy in small:
        copy.wait()
    fold[...] = y_ref[:, HALF:BACK_B].astype(F32)
    own = jnp.broadcast_to(fold[:, 0:1], (R8, T))
    picked = jnp.where(mix_ref[...].astype(F32) > 0.0, own, 0.0).reshape(E, SUB, T)
    ninth = jnp.broadcast_to(fold[pl.ds(0, E, stride=SUB), :][:, 1:2], (E, T))
    table = jnp.sum(picked, axis=1)
    table = table + jnp.where(sel9_ref[...].astype(F32) > 0.0, ninth, 0.0)
    expert = lax.broadcasted_iota(jnp.int32, (E, T), 0)
    totals = []
    for k in range(K):
        hit = ids_ref[k : k + 1, :] == expert
        totals.append(jnp.sum(jnp.where(hit, table, 0.0), axis=0, keepdims=True))
    gg_ref[...] = jnp.concatenate(totals, axis=0).astype(BF)
    send(gg_ref, gg_hbm)
    first.wait()
    for p in range(pieces):
        for copy in parts[p]:
            copy.wait()
        at = p * CN
        acc = part_ref[:, at : at + CN] + dot(sel_t_ref[...], y_ref[:, at : at + CN])
        out_ref[:, at : at + CN] = acc[0:T].astype(BF)
        out_ref[:, HALF + at : HALF + at + CN] = acc[T : 2 * T].astype(BF)
        for start in (at, HALF + at):
            cols = pl.ds(start, CN)
            send(out_ref.at[:, cols], out_hbm.at[:, cols])
    for store in stores:
        store.wait()


def combine_b(ids_t, mix, sel9, sel_t, part, y):
    return pl.pallas_call(
        combine_b_kernel,
        in_specs=[pl.BlockSpec(memory_space=pl.ANY)] * 6,
        out_specs=[pl.BlockSpec(memory_space=pl.ANY)] * 2,
        out_shape=[
            jax.ShapeDtypeStruct((T, D), BF),
            jax.ShapeDtypeStruct((K, T), BF),
        ],
        scratch_shapes=[
            pltpu.VMEM((K, T), jnp.int32),
            pltpu.VMEM((R8, T), BF),
            pltpu.VMEM((E, T), BF),
            pltpu.VMEM((2 * T, R8), BF),
            pltpu.VMEM((2 * T, HALF), F32),
            pltpu.VMEM((R8, BACK_B), BF),
            pltpu.VMEM((T, D), BF),
            pltpu.VMEM((K, T), BF),
            pltpu.VMEM((R8, LANE), F32),
            pltpu.SemaphoreType.DMA((7 + 2 * HALF // CN,)),
            pltpu.SemaphoreType.DMA((1 + 2 * HALF // CN,)),
        ],
        cost_estimate=cost(2 * R8 * T * D, 2 * R8 * BACK_B + 4 * T * D),
        name="combine_b",
    )(ids_t, mix, sel9, sel_t, part, y)


def exchange(x):
    width = x.shape[1]
    y = lax.all_to_all(
        x.reshape(E, SUB, width), AXES, split_axis=0, concat_axis=0, tiled=True
    )
    return y.reshape(R8, width)


def body(acts, out_grad, expert_ids, gate_vals, w_gate, w_up, w_down):
    ids_t = expert_ids.T
    gates_t = gate_vals.T
    wg, wu, wd = w_gate[0], w_up[0], w_down[0]
    send_a, sel_a, sel9, rank = pack_a(ids_t, gates_t, acts, out_grad)
    got_a = exchange(send_a)
    send_b, sel_b_t, mix = pack_b(rank, acts, out_grad)
    got_b = exchange(send_b)
    back_a, x_a, g_a, dpre_a, dup_a, hid_a, totals = expert_side(
        True, got_a, got_a, wg, wu, wd
    )
    wg_part = dot(x_a, dpre_a, 0, 0)
    wd_part = dot(hid_a, g_a, 0, 0)
    back_a, wg_part, wd_part = lax.optimization_barrier((back_a, wg_part, wd_part))
    home_a = exchange(back_a)
    back_b, x_b, g_b, dpre_b, dup_b, hid_b = expert_side(
        False, got_b, got_a, wg, wu, wd, totals
    )
    home_b = exchange(back_b)
    wg_grad = (wg_part + dot(x_b, dpre_b, 0, 0)).astype(BF)
    wu_grad = (dot(x_a, dup_a, 0, 0) + dot(x_b, dup_b, 0, 0)).astype(BF)
    wd_grad = (wd_part + dot(hid_b, g_b, 0, 0)).astype(BF)
    part = combine_a(sel_a, sel9, home_a)
    grad_acts, gate_grad_t = combine_b(ids_t, mix, sel9, sel_b_t, part, home_b)
    return (
        grad_acts,
        gate_grad_t.T,
        wg_grad[None],
        wu_grad[None],
        wd_grad[None],
    )


def solution(mesh):
    rows = P(AXES, None)
    mats = P(AXES, None, None)
    return jax.shard_map(
        body,
        mesh=mesh,
        in_specs=(rows, rows, rows, rows, mats, mats, mats),
        out_specs=(rows, rows, mats, mats, mats),
        check_vma=False,
    )
```
